32 devices in a mesh: section: 8 (over y, x, core), tok: 4 (over z).
Axes of the slice: x: 2, y: 2, z: 4, core: 2. Of those that a mesh axis runs over, the one named last changes fastest.
Arguments:
- carried_activations: bfloat16 [8, 512, 1536], P('section', 'tok'), may hold values from -6 to 6
- corrupted_field: bfloat16 [8, 512, 128], P('section', 'tok'), may hold values from -6 to 6
- gaussian_perturbation: bfloat16 [1, 512, 128], P(None, 'tok'), may hold values from -6 to 6
- timeline_entry_number: int32 [8], replicated, may hold values from 0 to 18
- ensemble_slots: int32 [8], replicated, may hold values from 0 to 7
- attention_entry_matrices: bfloat16 [8, 1536, 2304], P('section'), may hold values from -0.15625 to 0.15625
- attention_exit_matrix: bfloat16 [8, 768, 1536], P('section'), may hold values from -0.21875 to 0.21875
- adaptive_norm_terms: float32 [8, 20, 3, 1536], P('section'), may hold values from -3 to 3
- score_multiplier: float32 [8, 12], P('section'), may hold values from 0.5 to 30
- lifting_matrix: bfloat16 [128, 1536], replicated, may hold values from -0.5 to 0.5
- readout_matrix: bfloat16 [1536, 128], replicated, may hold values from -0.15625 to 0.15625
- ensemble_vectors: float32 [8, 1536], replicated, may hold values from -6 to 6
- denoiser_coefficients: float32 [20, 3], replicated, may hold values from 0.3 to 1
Outputs:
- hidden_out: bfloat16 [8, 512, 1536], P('section', 'tok')
- latent_out: bfloat16 [8, 512, 128], P('section', 'tok')
The draws below stay inside these ranges and needn't reach their ends.
Inputs may be any that keep to these rules, and one draw needn't show every extreme that they name: `timeline_entry_number`: listed by the section that holds the forecast at the start; the row advances by one each time the forecast passes the last layer. `ensemble_slots`: listed by the section that holds the forecast at the start.
All inputs are finite; a program needn't handle non-finite values.
Results may differ from the reference program's by a relative error of at most 0.0061.
Values may be sent and summed in bfloat16 or wider, within the bound.
A program may use at most 128 MiB of HBM per device.

```python
import math
import jax
import jax.numpy as jnp
from jax import lax

D = 1536
HEADS = 12
HD = 64
C = 128
SCHED = 20
ENSEMBLE = 8
DEPTH_TRAVERSALS = 1
MICRO = 8
LAYERS = 8
TOKENS = 512


def draw_score_multiplier(key, part):
    lower, upper = (0.5, 2.0)
    unit = jax.random.uniform(key, (LAYERS, HEADS), jnp.float32)
    return jnp.exp(jnp.log(lower) + unit * (jnp.log(upper) - jnp.log(lower)))


def set_ends(array, rng, least, high):
    dims = array.shape
    place = [jax.random.randint(jax.random.fold_in(rng, axis), (), 0, dims[axis]) for axis in range(len(dims))]
    array = array.at[tuple(place)].set(least)
    longest = dims.index(max(dims))
    place[longest] = (place[longest] + 1) % dims[longest]
    return array.at[tuple(place)].set(high)


def block_scale(own_key, shape, split, least, largest):
    gain = 1.0
    for axis_at, parts in split:
        steps = jax.random.uniform(jax.random.fold_in(jax.random.fold_in(own_key, 6), axis_at), (parts,), jnp.float32, least / len(split), largest / len(split))
        gain = gain * jnp.repeat(jnp.exp(steps), shape[axis_at] // parts).reshape((-1,) + (1,) * (len(shape) - 1 - axis_at))
    return gain


def scatter_about(rng, shape, spread, most, pieces=(), held_as=jnp.bfloat16):
    level = block_scale(rng, shape, pieces, -0.22, 0.18) if pieces else 1.0
    drawn = jax.random.normal(rng, shape, jnp.float32) * spread * level
    return jnp.minimum(jnp.maximum(drawn, -most), most).astype(held_as)


def setup_inputs(seed: int = 0) -> dict:
    arg_keys = jax.random.split(jax.random.key(seed), 14)
    return {
        "carried_activations": scatter_about(arg_keys[0], (MICRO, TOKENS, D), 1.0, 6.0, ((0, 8), (1, 4))),
        "corrupted_field": scatter_about(arg_keys[1], (MICRO, TOKENS, C), 1.0, 6.0, ((0, 8), (1, 4))),
        "gaussian_perturbation": scatter_about(arg_keys[2], (DEPTH_TRAVERSALS, TOKENS, C), 1.0, 6.0, ((1, 4),)),
        "timeline_entry_number": set_ends(jax.random.randint(arg_keys[3], (MICRO,), 0, SCHED - 1), jax.random.fold_in(arg_keys[3], 1), 0, (SCHED - 1) - 1).astype(jnp.int32),
        "ensemble_slots": set_ends(jax.random.randint(arg_keys[4], (MICRO,), 0, ENSEMBLE), jax.random.fold_in(arg_keys[4], 1), 0, ENSEMBLE - 1).astype(jnp.int32),
        "attention_entry_matrices": scatter_about(arg_keys[5], (LAYERS, D, 3 * HEADS * HD), D ** -0.5, 0.15625, ((0, 8),)),
        "attention_exit_matrix": scatter_about(arg_keys[6], (LAYERS, HEADS * HD, D), (HEADS * HD) ** -0.5, 0.21875, ((0, 8),)),
        "adaptive_norm_terms": scatter_about(arg_keys[7], (LAYERS, SCHED, 3, D), 0.5, 3.0, ((0, 8),), jnp.float32),
        "score_multiplier": draw_score_multiplier(jax.random.fold_in(arg_keys[13], 71), 0),
        "lifting_matrix": scatter_about(arg_keys[9], (C, D), C ** -0.5, 0.5),
        "readout_matrix": scatter_about(arg_keys[10], (D, C), D ** -0.5, 0.15625),
        "ensemble_vectors": scatter_about(arg_keys[11], (ENSEMBLE, D), 1.0, 6.0, (), jnp.float32),
        "denoiser_coefficients": jnp.clip(jax.random.uniform(arg_keys[12], (SCHED, 3), jnp.float32, 0.3, 1.0), 0.3, 1.0),
    }


def normalize(values):
    row_mean = lax.optimization_barrier(jnp.mean(values, axis=-1, keepdims=True))
    centred = values - row_mean
    row_var = lax.optimization_barrier(jnp.mean(centred * centred, axis=-1, keepdims=True))
    return centred * lax.rsqrt(row_var + 1e-06)

def head_attend(operands):
    queries, key_rows, value_rows, head_scale = operands
    scores = jnp.dot(queries, key_rows.T, preferred_element_type=jnp.float32) * head_scale
    row_top = lax.optimization_barrier(jnp.max(scores, axis=-1, keepdims=True))
    expd = jnp.exp(scores - row_top)
    row_sum = lax.optimization_barrier(jnp.sum(expd, axis=-1, keepdims=True))
    numer = jnp.dot(expd.astype(jnp.bfloat16), value_rows, preferred_element_type=jnp.float32)
    return numer / row_sum

def apply_depth_section(skip_connection_path, w_qkv_layer, w_out_layer, modulation_rows, head_temps):
    floats = skip_connection_path.astype(jnp.float32)
    modded = (normalize(floats) * (1.0 + modulation_rows[1]) + modulation_rows[0]).astype(jnp.bfloat16)
    joined_qkv = jnp.dot(modded, w_qkv_layer, preferred_element_type=jnp.float32).astype(jnp.bfloat16)
    attn_width = HEADS * HD
    local_rows = joined_qkv.shape[0]
    queries = joined_qkv[:, :attn_width].reshape(local_rows, HEADS, HD).transpose(1, 0, 2)
    key_rows = joined_qkv[:, attn_width:2 * attn_width].reshape(local_rows, HEADS, HD).transpose(1, 0, 2)
    value_rows = joined_qkv[:, 2 * attn_width:].reshape(local_rows, HEADS, HD).transpose(1, 0, 2)
    head_scale = head_temps / math.sqrt(HD)
    mixed = lax.map(head_attend, (queries, key_rows, value_rows, head_scale))
    attended = mixed.transpose(1, 0, 2).reshape(local_rows, attn_width).astype(jnp.bfloat16)
    branch = jnp.dot(attended, w_out_layer, preferred_element_type=jnp.float32)
    return (floats + modulation_rows[2] * branch).astype(jnp.bfloat16)

def rewrap(skip_connection_path, present_latent_field, noise_now, coefs, member_row, lifting_matrix, readout_matrix):
    normed_out = normalize(skip_connection_path.astype(jnp.float32)).astype(jnp.bfloat16)
    predicted = jnp.dot(normed_out, readout_matrix, preferred_element_type=jnp.float32)
    updated = (coefs[0] * present_latent_field.astype(jnp.float32) + coefs[1] * predicted + coefs[2] * noise_now.astype(jnp.float32)).astype(jnp.bfloat16)
    embedded = jnp.dot(updated, lifting_matrix, preferred_element_type=jnp.float32) + member_row
    return (embedded.astype(jnp.bfloat16), updated)

def reference(carried_activations, corrupted_field, gaussian_perturbation, timeline_entry_number, ensemble_slots, attention_entry_matrices, attention_exit_matrix, adaptive_norm_terms, score_multiplier, lifting_matrix, readout_matrix, ensemble_vectors, denoiser_coefficients):
    prediction_group = carried_activations.shape[0]
    concluding_results = [None] * prediction_group
    for ensemble_slot in range(prediction_group):
        skip_connection_path = carried_activations[ensemble_slot]
        present_latent_field = corrupted_field[ensemble_slot]
        timeline_entry_contents = timeline_entry_number[ensemble_slot]
        for clock_cycle_number in range(DEPTH_TRAVERSALS):
            depth_shift_amount = (ensemble_slot + clock_cycle_number) % prediction_group
            skip_connection_path = apply_depth_section(skip_connection_path, attention_entry_matrices[depth_shift_amount], attention_exit_matrix[depth_shift_amount], adaptive_norm_terms[depth_shift_amount, timeline_entry_contents], score_multiplier[depth_shift_amount])
            if depth_shift_amount == prediction_group - 1:
                skip_connection_path, present_latent_field = rewrap(skip_connection_path, present_latent_field, gaussian_perturbation[clock_cycle_number], denoiser_coefficients[timeline_entry_contents], ensemble_vectors[ensemble_slots[ensemble_slot]], lifting_matrix, readout_matrix)
                timeline_entry_contents = timeline_entry_contents + 1
        concluding_results[(ensemble_slot + DEPTH_TRAVERSALS) % prediction_group] = (skip_connection_path, present_latent_field)
    hidden_out = jnp.stack([pair[0] for pair in concluding_results])
    latent_out = jnp.stack([pair[1] for pair in concluding_results])
    return (hidden_out, latent_out)
```

```python
import functools
import math

import jax
import jax.numpy as jnp
from jax import lax
from jax.experimental import pallas as pl
from jax.experimental.pallas import tpu as pltpu
from jax.sharding import PartitionSpec as P

MESH = pl.DeviceIdType.MESH
F32 = jnp.float32
BF16 = jnp.bfloat16


def normalize(values):
    row_mean = jnp.mean(values, axis=-1, keepdims=True)
    centred = values - row_mean
    row_var = jnp.mean(centred * centred, axis=-1, keepdims=True)
    return centred * lax.rsqrt(row_var + 1e-06)


def line_kernel(
    n, sections, heads, chunks,
    rows_ref, slots_ref, mult_ref, coef_ref,
    x_hbm, state_hbm, noise_hbm, mods_hbm, ens_hbm,
    wqkv_ref, wout_ref, lift_ref, read_ref,
    h_ref, s_ref,
    w_buf, wout_buf, lift_buf, read_buf, xa, kv, qs, acc, top, total, att, ybuf, upd, q_out, q_in, o_out, o_in,
    x_ref, state_ref, noise_ref, mods_ref, ens_ref,
    local_sem, send_sem, recv_sem, out_send, out_recv, st_send, st_recv,
    q_send, q_recv, o_send, o_recv,
):
    sec = lax.axis_index("section")
    pos = lax.axis_index("tok")
    last = sections - 1
    nxt = lax.rem(sec + 1, sections)
    prev = lax.rem(sec + sections - 1, sections)
    local = x_hbm.shape[1]
    half = local // 2
    width = wout_ref.shape[1]
    model = x_hbm.shape[2]
    head_size = width // heads
    pairs = heads // 2
    lanes = 2 * head_size
    cols = model // chunks

    starts = (width, 2 * width, 0)
    w_copies = [
        pltpu.make_async_copy(
            wqkv_ref.at[0, :, pl.ds(starts[g], width)], w_buf.at[g], local_sem.at[g]
        )
        for g in range(3)
    ]
    rest = [
        pltpu.make_async_copy(wout_ref.at[0], wout_buf, local_sem.at[3]),
        pltpu.make_async_copy(lift_ref, lift_buf, local_sem.at[4]),
        pltpu.make_async_copy(read_ref, read_buf, local_sem.at[5]),
    ]
    small = [
        pltpu.make_async_copy(source_ref, target_ref, local_sem.at[6 + i])
        for i, (source_ref, target_ref) in enumerate(
            (
                (x_hbm, x_ref),
                (mods_hbm, mods_ref),
                (state_hbm, state_ref),
                (noise_hbm, noise_ref),
                (ens_hbm, ens_ref),
            )
        )
    ]
    for copy in small + w_copies + rest:
        copy.start()

    barrier = pltpu.get_barrier_semaphore()
    has_up = pos + 1 < n
    has_down = pos > 0

    @pl.when(has_up)
    def _():
        pl.semaphore_signal(barrier, inc=1, device_id=(sec, pos + 1), device_id_type=MESH)

    @pl.when(has_down)
    def _():
        pl.semaphore_signal(barrier, inc=1, device_id=(sec, pos - 1), device_id_type=MESH)

    pl.semaphore_signal(barrier, inc=1, device_id=(nxt, pos), device_id_type=MESH)
    pl.semaphore_signal(barrier, inc=1, device_id=(prev, pos), device_id_type=MESH)
    pl.semaphore_wait(barrier, 2 + has_up.astype(jnp.int32) + has_down.astype(jnp.int32))

    def hop(kind, way, dist, own):
        origin = pos - (dist - 1) if way == 0 else pos + (dist - 1)
        target = pos + 1 if way == 0 else pos - 1
        if kind == 0:
            dst = xa.at[origin]
            src = x_hbm.at[0, pl.ds(0, half), :] if own else dst
        else:
            dst = kv.at[1, origin]
            src = dst
        return pltpu.make_async_remote_copy(
            src_ref=src,
            dst_ref=dst,
            send_sem=send_sem.at[kind, way, dist - 1],
            recv_sem=recv_sem.at[kind, way, dist - 1],
            device_id=(sec, target),
            device_id_type=MESH,
        )

    def sends(way, dist):
        if way == 0:
            return jnp.logical_and(pos + 2 < n, pos - (dist - 1) >= 0)
        return jnp.logical_and(pos > 1, pos + (dist - 1) < n)

    def gets(way, dist):
        if way == 0:
            return jnp.logical_and(pos + 1 < n, pos - dist >= 0)
        return jnp.logical_and(pos > 0, pos + dist < n)

    def source(way, dist):
        return pos - dist if way == 0 else pos + dist

    def arrival(kind, way, dist):
        origin = source(way, dist)
        dst = xa.at[origin] if kind == 0 else kv.at[1, origin]
        return pltpu.make_async_remote_copy(
            src_ref=dst,
            dst_ref=dst,
            send_sem=send_sem.at[kind, way, dist - 1],
            recv_sem=recv_sem.at[kind, way, dist - 1],
            device_id=(sec, pos + 1 if way == 1 else pos - 1),
            device_id_type=MESH,
        )

    def start_own(kind):
        for way in range(2):
            @pl.when(sends(way, 1))
            def _():
                hop(kind, way, 1, True).start()

    start_own(0)

    state_copy = pltpu.make_async_remote_copy(
        src_ref=state_hbm.at[0],
        dst_ref=s_ref.at[0],
        send_sem=st_send,
        recv_sem=st_recv,
        device_id=(nxt, pos),
        device_id_type=MESH,
    )

    @pl.when(sec != last)
    def _():
        state_copy.start()

    small[0].wait()
    small[1].wait()
    plan = rows_ref[sec]
    shift = mods_ref[3 * plan + 0]
    scale = 1.0 + mods_ref[3 * plan + 1]
    gate = mods_ref[3 * plan + 2]

    def modulate(values):
        return (normalize(values.astype(F32)) * scale + shift).astype(BF16)

    modded = modulate(x_ref[0])
    for g in range(2):
        w_copies[g].wait()
        made = jnp.dot(modded, w_buf[g], preferred_element_type=F32).astype(BF16)
        kv[0, pos, :, g * width : (g + 1) * width] = made[:half]
        kv[1, pos, :, g * width : (g + 1) * width] = made[half:]
    start_own(1)
    w_copies[2].wait()
    queries = jnp.dot(modded, w_buf[2], preferred_element_type=F32)
    lane = lax.broadcasted_iota(jnp.int32, (local, lanes), 1)

    def spread(group, values):
        for pair in range(pairs):
            q_pair = values[:, pair * lanes : (pair + 1) * lanes]
            qs[group, pair, :local] = jnp.where(lane < head_size, q_pair, 0.0).astype(BF16)
            qs[group, pair, local:] = jnp.where(lane < head_size, 0.0, q_pair).astype(BF16)

    ends = ((0, 1), (n - 1, n - 2))
    at_end = jnp.logical_or(pos == 0, pos == n - 1)
    at_hub = jnp.logical_or(pos == 1, pos == n - 2)

    def query_copy(hub):
        return pltpu.make_async_remote_copy(
            src_ref=q_out,
            dst_ref=q_in,
            send_sem=q_send,
            recv_sem=q_recv,
            device_id=(sec, hub),
            device_id_type=MESH,
        )

    def mixed_copy(pair, end):
        return pltpu.make_async_remote_copy(
            src_ref=o_out.at[pair],
            dst_ref=o_in.at[pair],
            send_sem=o_send.at[pair],
            recv_sem=o_recv.at[pair],
            device_id=(sec, end),
            device_id_type=MESH,
        )

    @pl.when(at_end)
    def _():
        q_out[...] = queries.astype(BF16)

    for end, hub in ends:
        @pl.when(pos == end)
        def _():
            query_copy(hub).start()

    @pl.when(jnp.logical_not(at_end))
    def _():
        spread(0, queries)

    def take(kind, way, dist):
        @pl.when(gets(way, dist))
        def _():
            arrival(kind, way, dist).wait_recv()

        @pl.when(jnp.logical_and(gets(way, dist), sends(way, dist + 1)))
        def _():
            hop(kind, way, dist + 1, False).start()

    low_slot = lax.div(2 * pos, n)
    far_slot = (n - 1) * (1 - low_slot)

    def step(dist, carry):
        for way in range(2):
            take(0, way, dist)
        for way in range(2):
            @pl.when(gets(way, dist))
            def _():
                origin = source(way, dist)
                far = modulate(xa[origin])
                for g in range(2):
                    kv[0, origin, :, g * width : (g + 1) * width] = jnp.dot(
                        far, w_buf[g], preferred_element_type=F32
                    ).astype(BF16)

        for way in range(2):
            take(1, way, dist)

        return carry

    lax.fori_loop(1, n - 2, step, 0)

    upper = lax.broadcasted_iota(jnp.int32, (2 * local, 1), 0) < local

    def block(group, kind, pair):
        low = pair * lanes
        held = pl.ds(low_slot, n - 1) if kind == 0 else pl.ds(far_slot, 1)
        keys = kv[:, held, :, low : low + lanes].reshape(-1, lanes)
        values = kv[:, held, :, width + low : width + low + lanes].reshape(-1, lanes)
        factor = jnp.where(upper, mult_ref[0, 2 * pair], mult_ref[0, 2 * pair + 1])
        scores = lax.dot_general(
            qs[group, pair], keys, (((1,), (1,)), ((), ())), preferred_element_type=F32
        ) * (factor / math.sqrt(head_size))
        row_top = jnp.max(scores, axis=-1, keepdims=True)
        expd = jnp.exp(scores - row_top)
        row_sum = jnp.sum(expd, axis=-1, keepdims=True)
        mixed = jnp.dot(expd.astype(BF16), values, preferred_element_type=F32)
        return row_top, row_sum, mixed

    def first(group):
        for pair in range(pairs):
            row_top, row_sum, mixed = block(group, 0, pair)
            top[group, pair] = row_top
            total[group, pair] = row_sum
            acc[group, pair] = mixed

    def second(group, pair):
        row_top, row_sum, mixed = block(group, 1, pair)
        new_top = jnp.maximum(top[group, pair], row_top)
        before = jnp.exp(top[group, pair] - new_top)
        now = jnp.exp(row_top - new_top)
        row_sum = total[group, pair] * before + row_sum * now
        mixed = (acc[group, pair] * before + mixed * now) / row_sum
        return jnp.where(lane < head_size, mixed[:local], mixed[local:]).astype(BF16)

    @pl.when(jnp.logical_not(at_end))
    def _():
        first(0)

    @pl.when(at_hub)
    def _():
        query_copy(pos).wait_recv()
        spread(1, q_in[...].astype(F32))
        first(1)

    step(n - 2, 0)

    @pl.when(at_hub)
    def _():
        for group in (range(pairs // 2), range(pairs // 2, pairs)):
            for pair in group:
                o_out[pair] = second(1, pair)
            for end, hub in ends:
                @pl.when(pos == hub)
                def _():
                    for pair in group:
                        mixed_copy(pair, end).start()

    @pl.when(jnp.logical_not(at_end))
    def _():
        for pair in range(pairs):
            att[:, pair * lanes : (pair + 1) * lanes] = second(0, pair)

    @pl.when(at_end)
    def _():
        for pair in range(pairs):
            mixed_copy(pair, pos).wait_recv()
            att[:, pair * lanes : (pair + 1) * lanes] = o_in[pair]

    rest[0].wait()
    out_copies = []
    for c in range(chunks):
        span = slice(c * cols, (c + 1) * cols)
        branch = jnp.dot(att[...], wout_buf[:, span], preferred_element_type=F32)
        ybuf[c] = (x_ref[0, :, span].astype(F32) + gate[:, span] * branch).astype(BF16)
        copy = pltpu.make_async_remote_copy(
            src_ref=ybuf.at[c],
            dst_ref=h_ref.at[0, :, pl.ds(c * cols, cols)],
            send_sem=out_send.at[c],
            recv_sem=out_recv.at[c],
            device_id=(nxt, pos),
            device_id_type=MESH,
        )
        out_copies.append(copy)

        @pl.when(sec != last)
        def _():
            copy.start()

    for copy in rest[1:] + small[2:]:
        copy.wait()
    upd_copy = pltpu.make_async_remote_copy(
        src_ref=upd,
        dst_ref=s_ref.at[0],
        send_sem=st_send,
        recv_sem=st_recv,
        device_id=(nxt, pos),
        device_id_type=MESH,
    )

    @pl.when(sec == last)
    def _():
        stream = jnp.concatenate([ybuf[c] for c in range(chunks)], axis=1)
        normed = normalize(stream.astype(F32)).astype(BF16)
        predicted = jnp.dot(normed, read_buf[...], preferred_element_type=F32)
        upd[...] = (
            coef_ref[0, plan] * state_ref[0].astype(F32)
            + coef_ref[1, plan] * predicted
            + coef_ref[2, plan] * noise_ref[0].astype(F32)
        ).astype(BF16)
        upd_copy.start()

    state_copy.wait_recv()

    @pl.when(sec == 0)
    def _():
        member = ens_ref[pl.ds(slots_ref[last], 1), :]
        h_ref[0] = (
            jnp.dot(s_ref[0], lift_buf[...], preferred_element_type=F32) + member
        ).astype(BF16)

    @pl.when(sec != 0)
    def _():
        for copy in out_copies:
            copy.wait_recv()

    @pl.when(sec != last)
    def _():
        for copy in out_copies:
            copy.wait_send()

    state_copy.wait_send()

    def drain(dist, carry):
        for kind in range(2):
            for way in range(2):
                @pl.when(sends(way, dist))
                def _():
                    hop(kind, way, dist, False).wait_send()

        return carry

    lax.fori_loop(1, n, drain, 0)

    for end, hub in ends:
        @pl.when(pos == end)
        def _():
            query_copy(hub).wait_send()

        @pl.when(pos == hub)
        def _():
            for pair in range(pairs):
                mixed_copy(pair, end).wait_send()


def hub_kernel(
    n, sections, heads,
    rows_ref, slots_ref, mult_ref, coef_ref,
    x_hbm, state_hbm, noise_hbm, mods_hbm, ens_hbm,
    wqkv_ref, wout_ref, lift_ref, read_ref,
    h_ref, s_ref,
    w_buf, wout_buf, lift_buf, read_buf, xa, modded, kv, qs, o_out, att, ybuf, upd,
    x_ref, state_ref, noise_ref, mods_ref, ens_ref,
    local_sem, x_send, x_recv, o_send, o_recv, y_send, y_recv, st_send, st_recv,
):
    sec = lax.axis_index("section")
    pos = lax.axis_index("tok")
    last = sections - 1
    nxt = lax.rem(sec + 1, sections)
    prev = lax.rem(sec + sections - 1, sections)
    local = x_hbm.shape[1]
    half = local // 2
    width = wout_ref.shape[1]
    model = x_hbm.shape[2]
    head_size = width // heads
    pairs = heads // 2
    lanes = 2 * head_size
    peers = n - 1
    side = peers * half

    odd = lax.rem(sec, 2)
    place_of = odd * pos + (1 - odd) * (n - 1 - pos)
    hub = odd * 1 + (1 - odd) * (n - 2)
    at_hub = place_of == 1
    slot = lax.rem(place_of + 2, n)

    def peer(index):
        where = (index + 2) % n
        return odd * where + (1 - odd) * (n - 1 - where)

    w_copy = pltpu.make_async_copy(wqkv_ref.at[0], w_buf, local_sem.at[0])
    wout_copy = pltpu.make_async_copy(wout_ref.at[0], wout_buf, local_sem.at[1])
    first = [
        pltpu.make_async_copy(x_hbm, x_ref, local_sem.at[2]),
        pltpu.make_async_copy(mods_hbm, mods_ref, local_sem.at[3]),
    ]
    late = [
        pltpu.make_async_copy(lift_ref, lift_buf, local_sem.at[4]),
        pltpu.make_async_copy(read_ref, read_buf, local_sem.at[5]),
        pltpu.make_async_copy(state_hbm, state_ref, local_sem.at[6]),
        pltpu.make_async_copy(noise_hbm, noise_ref, local_sem.at[7]),
        pltpu.make_async_copy(ens_hbm, ens_ref, local_sem.at[8]),
    ]
    barrier = pltpu.get_barrier_semaphore()

    def greet(device):
        pl.semaphore_signal(barrier, inc=1, device_id=device, device_id_type=MESH)

    @pl.when(at_hub)
    def _():
        for index in range(peers):
            greet((sec, peer(index)))

    @pl.when(jnp.logical_not(at_hub))
    def _():
        greet((sec, hub))

    greet((nxt, pos))
    greet((prev, pos))
    for copy in first:
        copy.start()

    @pl.when(at_hub)
    def _():
        w_copy.start()

    for copy in [wout_copy] + late:
        copy.start()

    def x_copy(slot_at, piece):
        return pltpu.make_async_remote_copy(
            src_ref=modded.at[pl.ds(piece * half, half), :],
            dst_ref=xa.at[piece, slot_at],
            send_sem=x_send.at[piece],
            recv_sem=x_recv.at[piece, slot_at],
            device_id=(sec, hub),
            device_id_type=MESH,
        )

    def o_copy(piece, index, part):
        cols = pl.ds(part * (width // 2), width // 2)
        return pltpu.make_async_remote_copy(
            src_ref=o_out.at[piece, index, :, cols],
            dst_ref=att.at[pl.ds(piece * half, half), cols],
            send_sem=o_send.at[piece, index, part],
            recv_sem=o_recv.at[piece, part],
            device_id=(sec, peer(index)),
            device_id_type=MESH,
        )

    def y_copy(piece):
        return pltpu.make_async_remote_copy(
            src_ref=ybuf.at[pl.ds(piece * half, half), :],
            dst_ref=h_ref.at[0, pl.ds(piece * half, half), :],
            send_sem=y_send.at[piece],
            recv_sem=y_recv.at[piece],
            device_id=(nxt, pos),
            device_id_type=MESH,
        )

    state_copy = pltpu.make_async_remote_copy(
        src_ref=state_hbm.at[0],
        dst_ref=s_ref.at[0],
        send_sem=st_send,
        recv_sem=st_recv,
        device_id=(nxt, pos),
        device_id_type=MESH,
    )

    for copy in first:
        copy.wait()
    plan = rows_ref[sec]
    shift = mods_ref[3 * plan + 0]
    scale = 1.0 + mods_ref[3 * plan + 1]
    gate = mods_ref[3 * plan + 2]
    modded[...] = (normalize(x_ref[0].astype(F32)) * scale + shift).astype(BF16)

    @pl.when(jnp.logical_not(at_hub))
    def _():
        pl.semaphore_wait(barrier, 3)
        for piece in range(2):
            x_copy(slot, piece).start()

    @pl.when(at_hub)
    def _():
        pl.semaphore_wait(barrier, 2 + peers)

    @pl.when(sec != last)
    def _():
        state_copy.start()

    def branch_rows(piece, mixed):
        rows = slice(piece * half, (piece + 1) * half)
        branch = jnp.dot(mixed, wout_buf[...], preferred_element_type=F32)
        ybuf[rows, :] = (x_ref[0, rows, :].astype(F32) + gate * branch).astype(BF16)

        @pl.when(sec != last)
        def _():
            y_copy(piece).start()

    def project(rows, values):
        made = jnp.dot(values, w_buf[...], preferred_element_type=F32).astype(BF16)
        qs[rows, :] = made[:, :width]
        kv[rows, :] = made[:, width:]

    log2e = 1.0 / math.log(2.0)

    def attend(start, count, pair):
        low = pair * lanes
        lane = lax.broadcasted_iota(jnp.int32, (count, lanes), 1)
        query = qs[start : start + count, low : low + lanes]
        zero = jnp.zeros_like(query)
        stacked = jnp.concatenate(
            [jnp.where(lane < head_size, query, zero), jnp.where(lane < head_size, zero, query)],
            axis=0,
        )
        scores = lax.dot_general(
            stacked, kv[:, low : low + lanes], (((1,), (1,)), ((), ())), preferred_element_type=F32
        )
        expd, sums = [], []
        for one in range(2):
            part = scores[one * count : (one + 1) * count]
            factor = mult_ref[0, 2 * pair + one] * (log2e / math.sqrt(head_size))
            top = jnp.max(part, axis=-1, keepdims=True)
            weights = jnp.exp2(part * factor - top * factor)
            sums.append(jnp.sum(weights, axis=-1, keepdims=True))
            expd.append(weights.astype(BF16))
        mixed = jnp.dot(
            jnp.concatenate(expd, axis=0),
            kv[:, width + low : width + low + lanes],
            preferred_element_type=F32,
        )
        return jnp.where(
            lane < head_size, mixed[:count] / sums[0], mixed[count:] / sums[1]
        ).astype(BF16)

    @pl.when(at_hub)
    def _():
        w_copy.wait()
        project(slice(0, local), modded[...])
        for piece in range(2):
            for index in range(peers):
                x_copy(index, piece).wait_recv()
            start = local + piece * side
            project(slice(start, start + side), xa[piece].reshape(side, model))
        for piece in range(2):
            for part in range(2):
                for pair in range(part * pairs // 2, (part + 1) * pairs // 2):
                    mixed = attend(local + piece * side, side, pair)
                    for index in range(peers):
                        o_out[piece, index, :, pair * lanes : (pair + 1) * lanes] = mixed[
                            index * half : (index + 1) * half
                        ]
                for index in (1, 0, 2):
                    o_copy(piece, index, part).start()
        for pair in range(pairs):
            att[:, pair * lanes : (pair + 1) * lanes] = attend(0, local, pair)

    wout_copy.wait()
    for piece in range(2):
        @pl.when(jnp.logical_not(at_hub))
        def _():
            for part in range(2):
                o_copy(piece, 0, part).wait_recv()

        branch_rows(piece, att[piece * half : (piece + 1) * half, :])

    for copy in late:
        copy.wait()
    upd_copy = pltpu.make_async_remote_copy(
        src_ref=upd,
        dst_ref=s_ref.at[0],
        send_sem=st_send,
        recv_sem=st_recv,
        device_id=(nxt, pos),
        device_id_type=MESH,
    )

    @pl.when(sec == last)
    def _():
        normed = normalize(ybuf[...].astype(F32)).astype(BF16)
        predicted = jnp.dot(normed, read_buf[...], preferred_element_type=F32)
        upd[...] = (
            coef_ref[0, plan] * state_ref[0].astype(F32)
            + coef_ref[1, plan] * predicted
            + coef_ref[2, plan] * noise_ref[0].astype(F32)
        ).astype(BF16)
        upd_copy.start()

    state_copy.wait_recv()

    @pl.when(sec == 0)
    def _():
        member = ens_ref[pl.ds(slots_ref[last], 1), :]
        h_ref[0] = (
            jnp.dot(s_ref[0], lift_buf[...], preferred_element_type=F32) + member
        ).astype(BF16)

    @pl.when(sec != 0)
    def _():
        for piece in range(2):
            y_copy(piece).wait_recv()

    @pl.when(sec != last)
    def _():
        for piece in range(2):
            y_copy(piece).wait_send()

    state_copy.wait_send()

    @pl.when(at_hub)
    def _():
        for piece in range(2):
            for part in range(2):
                for index in range(peers):
                    o_copy(piece, index, part).wait_send()

    @pl.when(jnp.logical_not(at_hub))
    def _():
        for piece in range(2):
            x_copy(slot, piece).wait_send()


def place(pieces, h_in, s_in, h_out, s_out, h_buf, s_buf, in_sem, out_sem):
    size = h_in.shape[1] // pieces
    views = [(s_in.at[0], s_buf.at[0], s_out.at[0])] + [
        tuple(ref.at[0, pl.ds(i * size, size), :] for ref in (h_in, h_buf, h_out))
        for i in range(pieces)
    ]
    loads = [
        pltpu.make_async_copy(a, b, in_sem.at[i]) for i, (a, b, _) in enumerate(views)
    ]
    stores = [
        pltpu.make_async_copy(b, c, out_sem.at[i]) for i, (_, b, c) in enumerate(views)
    ]
    for copy in loads:
        copy.start()
    for load, store in zip(loads, stores):
        load.wait()
        store.start()
    for copy in stores:
        copy.wait()


def body(
    n, sections,
    carried_activations,
    corrupted_field,
    gaussian_perturbation,
    timeline_entry_number,
    ensemble_slots,
    attention_entry_matrices,
    attention_exit_matrix,
    adaptive_norm_terms,
    score_multiplier,
    lifting_matrix,
    readout_matrix,
    ensemble_vectors,
    denoiser_coefficients,
):
    _, local, model = carried_activations.shape
    channels = corrupted_field.shape[2]
    width = attention_exit_matrix.shape[1]
    heads = score_multiplier.shape[1]
    half = local // 2
    pairs = heads // 2
    lanes = 2 * (width // heads)
    chunks = 3
    terms = adaptive_norm_terms.reshape(-1, 1, model)
    smem = pl.BlockSpec(memory_space=pltpu.SMEM)
    vmem = pl.BlockSpec(memory_space=pltpu.VMEM)
    hbm = pl.BlockSpec(memory_space=pl.ANY)
    def dma(*shape):
        return pltpu.SemaphoreType.DMA(shape)

    staged = [
        pltpu.VMEM(carried_activations.shape, BF16),
        pltpu.VMEM(corrupted_field.shape, BF16),
        pltpu.VMEM(gaussian_perturbation.shape, BF16),
        pltpu.VMEM(terms.shape, F32),
        pltpu.VMEM(ensemble_vectors.shape, F32),
    ]
    if n == 4 and sections % 2 == 0 and heads % 4 == 0 and local % 32 == 0:
        run = functools.partial(hub_kernel, n, sections, heads)
        scratch = [
            pltpu.VMEM((model, 3 * width), BF16),
            pltpu.VMEM((width, model), BF16),
            pltpu.VMEM(lifting_matrix.shape, BF16),
            pltpu.VMEM(readout_matrix.shape, BF16),
            pltpu.VMEM((2, n - 1, half, model), BF16),
            pltpu.VMEM((local, model), BF16),
            pltpu.VMEM((n * local, 2 * width), BF16),
            pltpu.VMEM((n * local, width), BF16),
            pltpu.VMEM((2, n - 1, half, width), BF16),
            pltpu.VMEM((local, width), BF16),
            pltpu.VMEM((local, model), BF16),
            pltpu.VMEM((local, channels), BF16),
            *staged,
            dma(9), dma(2), dma(2, n - 1), dma(2, n - 1, 2), dma(2, 2), dma(2), dma(2),
            pltpu.SemaphoreType.DMA,
            pltpu.SemaphoreType.DMA,
        ]
    else:
        run = functools.partial(line_kernel, n, sections, heads, chunks)
        scratch = [
                pltpu.VMEM((3, model, width), BF16),
                pltpu.VMEM((width, model), BF16),
                pltpu.VMEM(lifting_matrix.shape, BF16),
                pltpu.VMEM(readout_matrix.shape, BF16),
                pltpu.VMEM((n, half, model), BF16),
                pltpu.VMEM((2, n, half, 2 * width), BF16),
                pltpu.VMEM((2, pairs, 2 * local, lanes), BF16),
                pltpu.VMEM((2, pairs, 2 * local, lanes), F32),
                pltpu.VMEM((2, pairs, 2 * local, 1), F32),
                pltpu.VMEM((2, pairs, 2 * local, 1), F32),
                pltpu.VMEM((local, width), BF16),
                pltpu.VMEM((chunks, local, model // chunks), BF16),
                pltpu.VMEM((local, channels), BF16),
                pltpu.VMEM((local, width), BF16),
                pltpu.VMEM((local, width), BF16),
                pltpu.VMEM((pairs, local, lanes), BF16),
                pltpu.VMEM((pairs, local, lanes), BF16),
                pltpu.VMEM(carried_activations.shape, BF16),
                pltpu.VMEM(corrupted_field.shape, BF16),
                pltpu.VMEM(gaussian_perturbation.shape, BF16),
                pltpu.VMEM(terms.shape, F32),
                pltpu.VMEM(ensemble_vectors.shape, F32),
                pltpu.SemaphoreType.DMA((11,)),
                pltpu.SemaphoreType.DMA((2, 2, n - 1)),
                pltpu.SemaphoreType.DMA((2, 2, n - 1)),
                pltpu.SemaphoreType.DMA((chunks,)),
                pltpu.SemaphoreType.DMA((chunks,)),
                pltpu.SemaphoreType.DMA,
                pltpu.SemaphoreType.DMA,
                pltpu.SemaphoreType.DMA,
                pltpu.SemaphoreType.DMA,
                pltpu.SemaphoreType.DMA((pairs,)),
                pltpu.SemaphoreType.DMA((pairs,)),
        ]
    stream, field = pl.pallas_call(
        run,
        out_shape=(
            jax.ShapeDtypeStruct(carried_activations.shape, BF16),
            jax.ShapeDtypeStruct(corrupted_field.shape, BF16),
        ),
        in_specs=[smem] * 4 + [hbm] * 9,
        out_specs=(vmem, vmem),
        scratch_shapes=scratch,
        compiler_params=pltpu.CompilerParams(
            collective_id=0, has_side_effects=True, vmem_limit_bytes=60 * 1024 * 1024
        ),
        name="denoise_pass",
    )(
        timeline_entry_number,
        ensemble_slots,
        score_multiplier,
        denoiser_coefficients.T,
        carried_activations,
        corrupted_field,
        gaussian_perturbation,
        terms,
        ensemble_vectors,
        attention_entry_matrices,
        attention_exit_matrix,
        lifting_matrix,
        readout_matrix,
    )
    pieces = 4
    return pl.pallas_call(
        functools.partial(place, pieces),
        out_shape=(
            jax.ShapeDtypeStruct(stream.shape, BF16),
            jax.ShapeDtypeStruct(field.shape, BF16),
        ),
        in_specs=[hbm, hbm],
        out_specs=(hbm, hbm),
        scratch_shapes=[
            pltpu.VMEM(stream.shape, BF16),
            pltpu.VMEM(field.shape, BF16),
            pltpu.SemaphoreType.DMA((pieces + 1,)),
            pltpu.SemaphoreType.DMA((pieces + 1,)),
        ],
        name="place_results",
    )(stream, field)


def solution(mesh):
    placed = (
        P("section", "tok", None),
        P("section", "tok", None),
        P(None, "tok", None),
        P(),
        P(),
        P("section", None, None),
        P("section", None, None),
        P("section", None, None, None),
        P("section", None),
        P(),
        P(),
        P(),
        P(),
    )
    return jax.shard_map(
        functools.partial(body, mesh.shape["tok"], mesh.shape["section"]),
        mesh=mesh,
        in_specs=placed,
        out_specs=(P("section", "tok", None), P("section", "tok", None)),
        check_vma=False,
    )
```

```python
import functools
import math

import jax
import jax.numpy as jnp
from jax import lax
from jax.experimental import pallas as pl
from jax.experimental.pallas import tpu as pltpu
from jax.sharding import PartitionSpec as P

MESH = pl.DeviceIdType.MESH
F32 = jnp.float32
BF16 = jnp.bfloat16


def normalize(values):
    row_mean = jnp.mean(values, axis=-1, keepdims=True)
    centred = values - row_mean
    row_var = jnp.mean(centred * centred, axis=-1, keepdims=True)
    return centred * lax.rsqrt(row_var + 1e-06)


def line_kernel(
    n, sections, heads, chunks,
    rows_ref, slots_ref, mult_ref, coef_ref,
    x_hbm, state_hbm, noise_hbm, mods_hbm, ens_hbm,
    wqkv_ref, wout_ref, lift_ref, read_ref,
    h_ref, s_ref,
    w_buf, wout_buf, lift_buf, read_buf, xa, kv, qs, acc, top, total, att, ybuf, upd, q_out, q_in, o_out, o_in,
    x_ref, state_ref, noise_ref, mods_ref, ens_ref,
    local_sem, send_sem, recv_sem, out_send, out_recv, st_send, st_recv,
    q_send, q_recv, o_send, o_recv,
):
    sec = lax.axis_index("section")
    pos = lax.axis_index("tok")
    last = sections - 1
    nxt = lax.rem(sec + 1, sections)
    prev = lax.rem(sec + sections - 1, sections)
    local = x_hbm.shape[1]
    half = local // 2
    width = wout_ref.shape[1]
    model = x_hbm.shape[2]
    head_size = width // heads
    pairs = heads // 2
    lanes = 2 * head_size
    cols = model // chunks

    starts = (width, 2 * width, 0)
    w_copies = [
        pltpu.make_async_copy(
            wqkv_ref.at[0, :, pl.ds(starts[g], width)], w_buf.at[g], local_sem.at[g]
        )
        for g in range(3)
    ]
    rest = [
        pltpu.make_async_copy(wout_ref.at[0], wout_buf, local_sem.at[3]),
        pltpu.make_async_copy(lift_ref, lift_buf, local_sem.at[4]),
        pltpu.make_async_copy(read_ref, read_buf, local_sem.at[5]),
    ]
    small = [
        pltpu.make_async_copy(source_ref, target_ref, local_sem.at[6 + i])
        for i, (source_ref, target_ref) in enumerate(
            (
                (x_hbm, x_ref),
                (mods_hbm, mods_ref),
                (state_hbm, state_ref),
                (noise_hbm, noise_ref),
                (ens_hbm, ens_ref),
            )
        )
    ]
    for copy in small + w_copies + rest:
        copy.start()

    barrier = pltpu.get_barrier_semaphore()
    has_up = pos + 1 < n
    has_down = pos > 0

    @pl.when(has_up)
    def _():
        pl.semaphore_signal(barrier, inc=1, device_id=(sec, pos + 1), device_id_type=MESH)

    @pl.when(has_down)
    def _():
        pl.semaphore_signal(barrier, inc=1, device_id=(sec, pos - 1), device_id_type=MESH)

    pl.semaphore_signal(barrier, inc=1, device_id=(nxt, pos), device_id_type=MESH)
    pl.semaphore_signal(barrier, inc=1, device_id=(prev, pos), device_id_type=MESH)
    pl.semaphore_wait(barrier, 2 + has_up.astype(jnp.int32) + has_down.astype(jnp.int32))

    def hop(kind, way, dist, own):
        origin = pos - (dist - 1) if way == 0 else pos + (dist - 1)
        target = pos + 1 if way == 0 else pos - 1
        if kind == 0:
            dst = xa.at[origin]
            src = x_hbm.at[0, pl.ds(0, half), :] if own else dst
        else:
            dst = kv.at[1, origin]
            src = dst
        return pltpu.make_async_remote_copy(
            src_ref=src,
            dst_ref=dst,
            send_sem=send_sem.at[kind, way, dist - 1],
            recv_sem=recv_sem.at[kind, way, dist - 1],
            device_id=(sec, target),
            device_id_type=MESH,
        )

    def sends(way, dist):
        if way == 0:
            return jnp.logical_and(pos + 2 < n, pos - (dist - 1) >= 0)
        return jnp.logical_and(pos > 1, pos + (dist - 1) < n)

    def gets(way, dist):
        if way == 0:
            return jnp.logical_and(pos + 1 < n, pos - dist >= 0)
        return jnp.logical_and(pos > 0, pos + dist < n)

    def source(way, dist):
        return pos - dist if way == 0 else pos + dist

    def arrival(kind, way, dist):
        origin = source(way, dist)
        dst = xa.at[origin] if kind == 0 else kv.at[1, origin]
        return pltpu.make_async_remote_copy(
            src_ref=dst,
            dst_ref=dst,
            send_sem=send_sem.at[kind, way, dist - 1],
            recv_sem=recv_sem.at[kind, way, dist - 1],
            device_id=(sec, pos + 1 if way == 1 else pos - 1),
            device_id_type=MESH,
        )

    def start_own(kind):
        for way in range(2):
            @pl.when(sends(way, 1))
            def _():
                hop(kind, way, 1, True).start()

    start_own(0)

    state_copy = pltpu.make_async_remote_copy(
        src_ref=state_hbm.at[0],
        dst_ref=s_ref.at[0],
        send_sem=st_send,
        recv_sem=st_recv,
        device_id=(nxt, pos),
        device_id_type=MESH,
    )

    @pl.when(sec != last)
    def _():
        state_copy.start()

    small[0].wait()
    small[1].wait()
    plan = rows_ref[sec]
    shift = mods_ref[3 * plan + 0]
    scale = 1.0 + mods_ref[3 * plan + 1]
    gate = mods_ref[3 * plan + 2]

    def modulate(values):
        return (normalize(values.astype(F32)) * scale + shift).astype(BF16)

    modded = modulate(x_ref[0])
    for g in range(2):
        w_copies[g].wait()
        made = jnp.dot(modded, w_buf[g], preferred_element_type=F32).astype(BF16)
        kv[0, pos, :, g * width : (g + 1) * width] = made[:half]
        kv[1, pos, :, g * width : (g + 1) * width] = made[half:]
    start_own(1)
    w_copies[2].wait()
    queries = jnp.dot(modded, w_buf[2], preferred_element_type=F32)
    lane = lax.broadcasted_iota(jnp.int32, (local, lanes), 1)

    def spread(group, values):
        for pair in range(pairs):
            q_pair = values[:, pair * lanes : (pair + 1) * lanes]
            qs[group, pair, :local] = jnp.where(lane < head_size, q_pair, 0.0).astype(BF16)
            qs[group, pair, local:] = jnp.where(lane < head_size, 0.0, q_pair).astype(BF16)

    ends = ((0, 1), (n - 1, n - 2))
    at_end = jnp.logical_or(pos == 0, pos == n - 1)
    at_hub = jnp.logical_or(pos == 1, pos == n - 2)

    def query_copy(hub):
        return pltpu.make_async_remote_copy(
            src_ref=q_out,
            dst_ref=q_in,
            send_sem=q_send,
            recv_sem=q_recv,
            device_id=(sec, hub),
            device_id_type=MESH,
        )

    def mixed_copy(pair, end):
        return pltpu.make_async_remote_copy(
            src_ref=o_out.at[pair],
            dst_ref=o_in.at[pair],
            send_sem=o_send.at[pair],
            recv_sem=o_recv.at[pair],
            device_id=(sec, end),
            device_id_type=MESH,
        )

    @pl.when(at_end)
    def _():
        q_out[...] = queries.astype(BF16)

    for end, hub in ends:
        @pl.when(pos == end)
        def _():
            query_copy(hub).start()

    @pl.when(jnp.logical_not(at_end))
    def _():
        spread(0, queries)

    def take(kind, way, dist):
        @pl.when(gets(way, dist))
        def _():
            arrival(kind, way, dist).wait_recv()

        @pl.when(jnp.logical_and(gets(way, dist), sends(way, dist + 1)))
        def _():
            hop(kind, way, dist + 1, False).start()

    low_slot = lax.div(2 * pos, n)
    far_slot = (n - 1) * (1 - low_slot)

    def step(dist, carry):
        for way in range(2):
            take(0, way, dist)
        for way in range(2):
            @pl.when(gets(way, dist))
            def _():
                origin = source(way, dist)
                far = modulate(xa[origin])
                for g in range(2):
                    kv[0, origin, :, g * width : (g + 1) * width] = jnp.dot(
                        far, w_buf[g], preferred_element_type=F32
                    ).astype(BF16)

        for way in range(2):
            take(1, way, dist)

        return carry

    lax.fori_loop(1, n - 2, step, 0)

    upper = lax.broadcasted_iota(jnp.int32, (2 * local, 1), 0) < local

    def block(group, kind, pair):
        low = pair * lanes
        held = pl.ds(low_slot, n - 1) if kind == 0 else pl.ds(far_slot, 1)
        keys = kv[:, held, :, low : low + lanes].reshape(-1, lanes)
        values = kv[:, held, :, width + low : width + low + lanes].reshape(-1, lanes)
        factor = jnp.where(upper, mult_ref[0, 2 * pair], mult_ref[0, 2 * pair + 1])
        scores = lax.dot_general(
            qs[group, pair], keys, (((1,), (1,)), ((), ())), preferred_element_type=F32
        ) * (factor / math.sqrt(head_size))
        row_top = jnp.max(scores, axis=-1, keepdims=True)
        expd = jnp.exp(scores - row_top)
        row_sum = jnp.sum(expd, axis=-1, keepdims=True)
        mixed = jnp.dot(expd.astype(BF16), values, preferred_element_type=F32)
        return row_top, row_sum, mixed

    def first(group):
        for pair in range(pairs):
            row_top, row_sum, mixed = block(group, 0, pair)
            top[group, pair] = row_top
            total[group, pair] = row_sum
            acc[group, pair] = mixed

    def second(group, pair):
        row_top, row_sum, mixed = block(group, 1, pair)
        new_top = jnp.maximum(top[group, pair], row_top)
        before = jnp.exp(top[group, pair] - new_top)
        now = jnp.exp(row_top - new_top)
        row_sum = total[group, pair] * before + row_sum * now
        mixed = (acc[group, pair] * before + mixed * now) / row_sum
        return jnp.where(lane < head_size, mixed[:local], mixed[local:]).astype(BF16)

    @pl.when(jnp.logical_not(at_end))
    def _():
        first(0)

    @pl.when(at_hub)
    def _():
        query_copy(pos).wait_recv()
        spread(1, q_in[...].astype(F32))
        first(1)

    step(n - 2, 0)

    @pl.when(at_hub)
    def _():
        for group in (range(pairs // 2), range(pairs // 2, pairs)):
            for pair in group:
                o_out[pair] = second(1, pair)
            for end, hub in ends:
                @pl.when(pos == hub)
                def _():
                    for pair in group:
                        mixed_copy(pair, end).start()

    @pl.when(jnp.logical_not(at_end))
    def _():
        for pair in range(pairs):
            att[:, pair * lanes : (pair + 1) * lanes] = second(0, pair)

    @pl.when(at_end)
    def _():
        for pair in range(pairs):
            mixed_copy(pair, pos).wait_recv()
            att[:, pair * lanes : (pair + 1) * lanes] = o_in[pair]

    rest[0].wait()
    out_copies = []
    for c in range(chunks):
        span = slice(c * cols, (c + 1) * cols)
        branch = jnp.dot(att[...], wout_buf[:, span], preferred_element_type=F32)
        ybuf[c] = (x_ref[0, :, span].astype(F32) + gate[:, span] * branch).astype(BF16)
        copy = pltpu.make_async_remote_copy(
            src_ref=ybuf.at[c],
            dst_ref=h_ref.at[0, :, pl.ds(c * cols, cols)],
            send_sem=out_send.at[c],
            recv_sem=out_recv.at[c],
            device_id=(nxt, pos),
            device_id_type=MESH,
        )
        out_copies.append(copy)

        @pl.when(sec != last)
        def _():
            copy.start()

    for copy in rest[1:] + small[2:]:
        copy.wait()
    upd_copy = pltpu.make_async_remote_copy(
        src_ref=upd,
        dst_ref=s_ref.at[0],
        send_sem=st_send,
        recv_sem=st_recv,
        device_id=(nxt, pos),
        device_id_type=MESH,
    )

    @pl.when(sec == last)
    def _():
        stream = jnp.concatenate([ybuf[c] for c in range(chunks)], axis=1)
        normed = normalize(stream.astype(F32)).astype(BF16)
        predicted = jnp.dot(normed, read_buf[...], preferred_element_type=F32)
        upd[...] = (
            coef_ref[0, plan] * state_ref[0].astype(F32)
            + coef_ref[1, plan] * predicted
            + coef_ref[2, plan] * noise_ref[0].astype(F32)
        ).astype(BF16)
        upd_copy.start()

    state_copy.wait_recv()

    @pl.when(sec == 0)
    def _():
        member = ens_ref[pl.ds(slots_ref[last], 1), :]
        h_ref[0] = (
            jnp.dot(s_ref[0], lift_buf[...], preferred_element_type=F32) + member
        ).astype(BF16)

    @pl.when(sec != 0)
    def _():
        for copy in out_copies:
            copy.wait_recv()

    @pl.when(sec != last)
    def _():
        for copy in out_copies:
            copy.wait_send()

    state_copy.wait_send()

    def drain(dist, carry):
        for kind in range(2):
            for way in range(2):
                @pl.when(sends(way, dist))
                def _():
                    hop(kind, way, dist, False).wait_send()

        return carry

    lax.fori_loop(1, n, drain, 0)

    for end, hub in ends:
        @pl.when(pos == end)
        def _():
            query_copy(hub).wait_send()

        @pl.when(pos == hub)
        def _():
            for pair in range(pairs):
                mixed_copy(pair, end).wait_send()


def hub_kernel(
    n, sections, heads,
    rows_ref, slots_ref, mult_ref, coef_ref,
    x_hbm, state_hbm, noise_hbm, mods_hbm, ens_hbm,
    wqkv_ref, wout_ref, lift_ref, read_ref,
    h_ref, s_ref,
    w_buf, wout_buf, lift_buf, read_buf, xa, modded, kv, qs, o_out, att, ybuf, upd,
    x_ref, state_ref, noise_ref, mods_ref, ens_ref,
    local_sem, x_send, x_recv, o_send, o_recv, y_send, y_recv, st_send, st_recv,
):
    sec = lax.axis_index("section")
    pos = lax.axis_index("tok")
    last = sections - 1
    nxt = lax.rem(sec + 1, sections)
    prev = lax.rem(sec + sections - 1, sections)
    local = x_hbm.shape[1]
    half = local // 2
    width = wout_ref.shape[1]
    model = x_hbm.shape[2]
    head_size = width // heads
    pairs = heads // 2
    lanes = 2 * head_size
    peers = n - 1
    side = peers * half

    odd = lax.rem(sec, 2)
    place_of = odd * pos + (1 - odd) * (n - 1 - pos)
    hub = odd * 1 + (1 - odd) * (n - 2)
    at_hub = place_of == 1
    slot = lax.rem(place_of + 2, n)

    def peer(index):
        where = (index + 2) % n
        return odd * where + (1 - odd) * (n - 1 - where)

    w_copy = pltpu.make_async_copy(wqkv_ref.at[0], w_buf, local_sem.at[0])
    wout_copy = pltpu.make_async_copy(wout_ref.at[0], wout_buf, local_sem.at[1])
    first = [
        pltpu.make_async_copy(x_hbm, x_ref, local_sem.at[2]),
        pltpu.make_async_copy(mods_hbm, mods_ref, local_sem.at[3]),
    ]
    late = [
        pltpu.make_async_copy(lift_ref, lift_buf, local_sem.at[4]),
        pltpu.make_async_copy(read_ref, read_buf, local_sem.at[5]),
        pltpu.make_async_copy(state_hbm, state_ref, local_sem.at[6]),
        pltpu.make_async_copy(noise_hbm, noise_ref, local_sem.at[7]),
        pltpu.make_async_copy(ens_hbm, ens_ref, local_sem.at[8]),
    ]
    barrier = pltpu.get_barrier_semaphore()

    def greet(device):
        pl.semaphore_signal(barrier, inc=1, device_id=device, device_id_type=MESH)

    @pl.when(at_hub)
    def _():
        for index in range(peers):
            greet((sec, peer(index)))

    @pl.when(jnp.logical_not(at_hub))
    def _():
        greet((sec, hub))

    greet((nxt, pos))
    greet((prev, pos))
    for copy in first:
        copy.start()

    @pl.when(at_hub)
    def _():
        w_copy.start()

    for copy in [wout_copy] + late:
        copy.start()

    def x_copy(slot_at, piece):
        return pltpu.make_async_remote_copy(
            src_ref=modded.at[pl.ds(piece * half, half), :],
            dst_ref=xa.at[piece, slot_at],
            send_sem=x_send.at[piece],
            recv_sem=x_recv.at[piece, slot_at],
            device_id=(sec, hub),
            device_id_type=MESH,
        )

    def o_copy(piece, index, part):
        cols = pl.ds(part * (width // 2), width // 2)
        return pltpu.make_async_remote_copy(
            src_ref=o_out.at[piece, index, :, cols],
            dst_ref=att.at[pl.ds(piece * half, half), cols],
            send_sem=o_send.at[piece, index, part],
            recv_sem=o_recv.at[piece, part],
            device_id=(sec, peer(index)),
            device_id_type=MESH,
        )

    def y_copy(piece):
        return pltpu.make_async_remote_copy(
            src_ref=ybuf.at[pl.ds(piece * half, half), :],
            dst_ref=h_ref.at[0, pl.ds(piece * half, half), :],
            send_sem=y_send.at[piece],
            recv_sem=y_recv.at[piece],
            device_id=(nxt, pos),
            device_id_type=MESH,
        )

    state_copy = pltpu.make_async_remote_copy(
        src_ref=state_hbm.at[0],
        dst_ref=s_ref.at[0],
        send_sem=st_send,
        recv_sem=st_recv,
        device_id=(nxt, pos),
        device_id_type=MESH,
    )

    for copy in first:
        copy.wait()
    plan = rows_ref[sec]
    shift = mods_ref[3 * plan + 0]
    scale = 1.0 + mods_ref[3 * plan + 1]
    gate = mods_ref[3 * plan + 2]
    modded[...] = (normalize(x_ref[0].astype(F32)) * scale + shift).astype(BF16)

    @pl.when(jnp.logical_not(at_hub))
    def _():
        pl.semaphore_wait(barrier, 3)
        for piece in range(2):
            x_copy(slot, piece).start()

    @pl.when(at_hub)
    def _():
        pl.semaphore_wait(barrier, 2 + peers)

    @pl.when(sec != last)
    def _():
        state_copy.start()

    def branch_rows(piece, mixed):
        rows = slice(piece * half, (piece + 1) * half)
        branch = jnp.dot(mixed, wout_buf[...], preferred_element_type=F32)
        ybuf[rows, :] = (x_ref[0, rows, :].astype(F32) + gate * branch).astype(BF16)

        @pl.when(sec != last)
        def _():
            y_copy(piece).start()

    def project(rows, values):
        made = jnp.dot(values, w_buf[...], preferred_element_type=F32).astype(BF16)
        qs[rows, :] = made[:, :width]
        kv[rows, :] = made[:, width:]

    log2e = 1.0 / math.log(2.0)

    def attend(start, count, pair):
        low = pair * lanes
        lane = lax.broadcasted_iota(jnp.int32, (count, lanes), 1)
        query = qs[start : start + count, low : low + lanes]
        zero = jnp.zeros_like(query)
        stacked = jnp.concatenate(
            [jnp.where(lane < head_size, query, zero), jnp.where(lane < head_size, zero, query)],
            axis=0,
        )
        scores = lax.dot_general(
            stacked, kv[:, low : low + lanes], (((1,), (1,)), ((), ())), preferred_element_type=F32
        )
        expd, sums = [], []
        for one in range(2):
            part = scores[one * count : (one + 1) * count]
            factor = mult_ref[0, 2 * pair + one] * (log2e / math.sqrt(head_size))
            top = jnp.max(part, axis=-1, keepdims=True)
            weights = jnp.exp2(part * factor - top * factor)
            sums.append(jnp.sum(weights, axis=-1, keepdims=True))
            expd.append(weights.astype(BF16))
        mixed = jnp.dot(
            jnp.concatenate(expd, axis=0),
            kv[:, width + low : width + low + lanes],
            preferred_element_type=F32,
        )
        return jnp.where(
            lane < head_size, mixed[:count] / sums[0], mixed[count:] / sums[1]
        ).astype(BF16)

    @pl.when(at_hub)
    def _():
        w_copy.wait()
        project(slice(0, local), modded[...])
        for piece in range(2):
            for index in range(peers):
                x_copy(index, piece).wait_recv()
            start = local + piece * side
            project(slice(start, start + side), xa[piece].reshape(side, model))
        for piece in range(2):
            for part in range(2):
                for pair in range(part * pairs // 2, (part + 1) * pairs // 2):
                    mixed = attend(local + piece * side, side, pair)
                    for index in range(peers):
                        o_out[piece, index, :, pair * lanes : (pair + 1) * lanes] = mixed[
                            index * half : (index + 1) * half
                        ]
                for index in (1, 0, 2):
                    o_copy(piece, index, part).start()
        for pair in range(pairs):
            att[:, pair * lanes : (pair + 1) * lanes] = attend(0, local, pair)

    wout_copy.wait()
    for piece in range(2):
        @pl.when(jnp.logical_not(at_hub))
        def _():
            for part in range(2):
                o_copy(piece, 0, part).wait_recv()

        branch_rows(piece, att[piece * half : (piece + 1) * half, :])

    for copy in late:
        copy.wait()
    upd_copy = pltpu.make_async_remote_copy(
        src_ref=upd,
        dst_ref=s_ref.at[0],
        send_sem=st_send,
        recv_sem=st_recv,
        device_id=(nxt, pos),
        device_id_type=MESH,
    )

    @pl.when(sec == last)
    def _():
        normed = normalize(ybuf[...].astype(F32)).astype(BF16)
        predicted = jnp.dot(normed, read_buf[...], preferred_element_type=F32)
        upd[...] = (
            coef_ref[0, plan] * state_ref[0].astype(F32)
            + coef_ref[1, plan] * predicted
            + coef_ref[2, plan] * noise_ref[0].astype(F32)
        ).astype(BF16)
        upd_copy.start()

    state_copy.wait_recv()

    @pl.when(sec == 0)
    def _():
        member = ens_ref[pl.ds(slots_ref[last], 1), :]
        h_ref[0] = (
            jnp.dot(s_ref[0], lift_buf[...], preferred_element_type=F32) + member
        ).astype(BF16)

    @pl.when(sec != 0)
    def _():
        for piece in range(2):
            y_copy(piece).wait_recv()

    @pl.when(sec != last)
    def _():
        for piece in range(2):
            y_copy(piece).wait_send()

    state_copy.wait_send()

    @pl.when(at_hub)
    def _():
        for piece in range(2):
            for part in range(2):
                for index in range(peers):
                    o_copy(piece, index, part).wait_send()

    @pl.when(jnp.logical_not(at_hub))
    def _():
        for piece in range(2):
            x_copy(slot, piece).wait_send()


def place(h_in, s_in, h_out, s_out, sem):
    copies = [
        pltpu.make_async_copy(h_in, h_out, sem.at[0]),
        pltpu.make_async_copy(s_in, s_out, sem.at[1]),
    ]
    for copy in copies:
        copy.start()
    for copy in copies:
        copy.wait()


def body(
    n, sections,
    carried_activations,
    corrupted_field,
    gaussian_perturbation,
    timeline_entry_number,
    ensemble_slots,
    attention_entry_matrices,
    attention_exit_matrix,
    adaptive_norm_terms,
    score_multiplier,
    lifting_matrix,
    readout_matrix,
    ensemble_vectors,
    denoiser_coefficients,
):
    _, local, model = carried_activations.shape
    channels = corrupted_field.shape[2]
    width = attention_exit_matrix.shape[1]
    heads = score_multiplier.shape[1]
    half = local // 2
    pairs = heads // 2
    lanes = 2 * (width // heads)
    chunks = 3
    terms = adaptive_norm_terms.reshape(-1, 1, model)
    smem = pl.BlockSpec(memory_space=pltpu.SMEM)
    vmem = pl.BlockSpec(memory_space=pltpu.VMEM)
    hbm = pl.BlockSpec(memory_space=pl.ANY)
    def dma(*shape):
        return pltpu.SemaphoreType.DMA(shape)

    staged = [
        pltpu.VMEM(carried_activations.shape, BF16),
        pltpu.VMEM(corrupted_field.shape, BF16),
        pltpu.VMEM(gaussian_perturbation.shape, BF16),
        pltpu.VMEM(terms.shape, F32),
        pltpu.VMEM(ensemble_vectors.shape, F32),
    ]
    if n == 4 and sections % 2 == 0 and heads % 4 == 0 and local % 32 == 0:
        run = functools.partial(hub_kernel, n, sections, heads)
        scratch = [
            pltpu.VMEM((model, 3 * width), BF16),
            pltpu.VMEM((width, model), BF16),
            pltpu.VMEM(lifting_matrix.shape, BF16),
            pltpu.VMEM(readout_matrix.shape, BF16),
            pltpu.VMEM((2, n - 1, half, model), BF16),
            pltpu.VMEM((local, model), BF16),
            pltpu.VMEM((n * local, 2 * width), BF16),
            pltpu.VMEM((n * local, width), BF16),
            pltpu.VMEM((2, n - 1, half, width), BF16),
            pltpu.VMEM((local, width), BF16),
            pltpu.VMEM((local, model), BF16),
            pltpu.VMEM((local, channels), BF16),
            *staged,
            dma(9), dma(2), dma(2, n - 1), dma(2, n - 1, 2), dma(2, 2), dma(2), dma(2),
            pltpu.SemaphoreType.DMA,
            pltpu.SemaphoreType.DMA,
        ]
    else:
        run = functools.partial(line_kernel, n, sections, heads, chunks)
        scratch = [
                pltpu.VMEM((3, model, width), BF16),
                pltpu.VMEM((width, model), BF16),
                pltpu.VMEM(lifting_matrix.shape, BF16),
                pltpu.VMEM(readout_matrix.shape, BF16),
                pltpu.VMEM((n, half, model), BF16),
                pltpu.VMEM((2, n, half, 2 * width), BF16),
                pltpu.VMEM((2, pairs, 2 * local, lanes), BF16),
                pltpu.VMEM((2, pairs, 2 * local, lanes), F32),
                pltpu.VMEM((2, pairs, 2 * local, 1), F32),
                pltpu.VMEM((2, pairs, 2 * local, 1), F32),
                pltpu.VMEM((local, width), BF16),
                pltpu.VMEM((chunks, local, model // chunks), BF16),
                pltpu.VMEM((local, channels), BF16),
                pltpu.VMEM((local, width), BF16),
                pltpu.VMEM((local, width), BF16),
                pltpu.VMEM((pairs, local, lanes), BF16),
                pltpu.VMEM((pairs, local, lanes), BF16),
                pltpu.VMEM(carried_activations.shape, BF16),
                pltpu.VMEM(corrupted_field.shape, BF16),
                pltpu.VMEM(gaussian_perturbation.shape, BF16),
                pltpu.VMEM(terms.shape, F32),
                pltpu.VMEM(ensemble_vectors.shape, F32),
                pltpu.SemaphoreType.DMA((11,)),
                pltpu.SemaphoreType.DMA((2, 2, n - 1)),
                pltpu.SemaphoreType.DMA((2, 2, n - 1)),
                pltpu.SemaphoreType.DMA((chunks,)),
                pltpu.SemaphoreType.DMA((chunks,)),
                pltpu.SemaphoreType.DMA,
                pltpu.SemaphoreType.DMA,
                pltpu.SemaphoreType.DMA,
                pltpu.SemaphoreType.DMA,
                pltpu.SemaphoreType.DMA((pairs,)),
                pltpu.SemaphoreType.DMA((pairs,)),
        ]
    stream, field = pl.pallas_call(
        run,
        out_shape=(
            pltpu.VMEM(carried_activations.shape, BF16),
            pltpu.VMEM(corrupted_field.shape, BF16),
        ),
        in_specs=[smem] * 4 + [hbm] * 9,
        out_specs=(vmem, vmem),
        scratch_shapes=scratch,
        compiler_params=pltpu.CompilerParams(
            collective_id=0, has_side_effects=True, vmem_limit_bytes=60 * 1024 * 1024
        ),
        name="denoise_pass",
    )(
        timeline_entry_number,
        ensemble_slots,
        score_multiplier,
        denoiser_coefficients.T,
        carried_activations,
        corrupted_field,
        gaussian_perturbation,
        terms,
        ensemble_vectors,
        attention_entry_matrices,
        attention_exit_matrix,
        lifting_matrix,
        readout_matrix,
    )
    return pl.pallas_call(
        place,
        out_shape=(
            jax.ShapeDtypeStruct(stream.shape, BF16),
            jax.ShapeDtypeStruct(field.shape, BF16),
        ),
        in_specs=[vmem, vmem],
        out_specs=(hbm, hbm),
        scratch_shapes=[pltpu.SemaphoreType.DMA((2,))],
        name="place_results",
    )(
        pltpu.with_memory_space_constraint(stream, pltpu.VMEM),
        pltpu.with_memory_space_constraint(field, pltpu.VMEM),
    )


def solution(mesh):
    placed = (
        P("section", "tok", None),
        P("section", "tok", None),
        P(None, "tok", None),
        P(),
        P(),
        P("section", None, None),
        P("section", None, None),
        P("section", None, None, None),
        P("section", None),
        P(),
        P(),
        P(),
        P(),
    )
    return jax.shard_map(
        functools.partial(body, mesh.shape["tok"], mesh.shape["section"]),
        mesh=mesh,
        in_specs=placed,
        out_specs=(P("section", "tok", None), P("section", "tok", None)),
        check_vma=False,
    )
```

```python
import functools
import math

import jax
import jax.numpy as jnp
from jax import lax
from jax.experimental import pallas as pl
from jax.experimental.pallas import tpu as pltpu
from jax.sharding import PartitionSpec as P

MESH = pl.DeviceIdType.MESH
F32 = jnp.float32
BF16 = jnp.bfloat16


def normalize(values):
    row_mean = jnp.mean(values, axis=-1, keepdims=True)
    centred = values - row_mean
    row_var = jnp.mean(centred * centred, axis=-1, keepdims=True)
    return centred * lax.rsqrt(row_var + 1e-06)


def line_kernel(
    n, sections, heads, chunks,
    rows_ref, slots_ref, mult_ref, coef_ref,
    x_hbm, state_hbm, noise_hbm, mods_hbm, ens_hbm,
    wqkv_ref, wout_ref, lift_ref, read_ref,
    h_ref, s_ref,
    w_buf, wout_buf, lift_buf, read_buf, xa, kv, qs, acc, top, total, att, ybuf, upd, q_out, q_in, o_out, o_in,
    x_ref, state_ref, noise_ref, mods_ref, ens_ref,
    local_sem, send_sem, recv_sem, out_send, out_recv, st_send, st_recv,
    q_send, q_recv, o_send, o_recv,
):
    sec = lax.axis_index("section")
    pos = lax.axis_index("tok")
    last = sections - 1
    nxt = lax.rem(sec + 1, sections)
    prev = lax.rem(sec + sections - 1, sections)
    local = x_hbm.shape[1]
    half = local // 2
    width = wout_ref.shape[1]
    model = x_hbm.shape[2]
    head_size = width // heads
    pairs = heads // 2
    lanes = 2 * head_size
    cols = model // chunks

    starts = (width, 2 * width, 0)
    w_copies = [
        pltpu.make_async_copy(
            wqkv_ref.at[0, :, pl.ds(starts[g], width)], w_buf.at[g], local_sem.at[g]
        )
        for g in range(3)
    ]
    rest = [
        pltpu.make_async_copy(wout_ref.at[0], wout_buf, local_sem.at[3]),
        pltpu.make_async_copy(lift_ref, lift_buf, local_sem.at[4]),
        pltpu.make_async_copy(read_ref, read_buf, local_sem.at[5]),
    ]
    small = [
        pltpu.make_async_copy(source_ref, target_ref, local_sem.at[6 + i])
        for i, (source_ref, target_ref) in enumerate(
            (
                (x_hbm, x_ref),
                (mods_hbm, mods_ref),
                (state_hbm, state_ref),
                (noise_hbm, noise_ref),
                (ens_hbm, ens_ref),
            )
        )
    ]
    for copy in small + w_copies + rest:
        copy.start()

    barrier = pltpu.get_barrier_semaphore()
    has_up = pos + 1 < n
    has_down = pos > 0

    @pl.when(has_up)
    def _():
        pl.semaphore_signal(barrier, inc=1, device_id=(sec, pos + 1), device_id_type=MESH)

    @pl.when(has_down)
    def _():
        pl.semaphore_signal(barrier, inc=1, device_id=(sec, pos - 1), device_id_type=MESH)

    pl.semaphore_signal(barrier, inc=1, device_id=(nxt, pos), device_id_type=MESH)
    pl.semaphore_signal(barrier, inc=1, device_id=(prev, pos), device_id_type=MESH)
    pl.semaphore_wait(barrier, 2 + has_up.astype(jnp.int32) + has_down.astype(jnp.int32))

    def hop(kind, way, dist, own):
        origin = pos - (dist - 1) if way == 0 else pos + (dist - 1)
        target = pos + 1 if way == 0 else pos - 1
        if kind == 0:
            dst = xa.at[origin]
            src = x_hbm.at[0, pl.ds(0, half), :] if own else dst
        else:
            dst = kv.at[1, origin]
            src = dst
        return pltpu.make_async_remote_copy(
            src_ref=src,
            dst_ref=dst,
            send_sem=send_sem.at[kind, way, dist - 1],
            recv_sem=recv_sem.at[kind, way, dist - 1],
            device_id=(sec, target),
            device_id_type=MESH,
        )

    def sends(way, dist):
        if way == 0:
            return jnp.logical_and(pos + 2 < n, pos - (dist - 1) >= 0)
        return jnp.logical_and(pos > 1, pos + (dist - 1) < n)

    def gets(way, dist):
        if way == 0:
            return jnp.logical_and(pos + 1 < n, pos - dist >= 0)
        return jnp.logical_and(pos > 0, pos + dist < n)

    def source(way, dist):
        return pos - dist if way == 0 else pos + dist

    def arrival(kind, way, dist):
        origin = source(way, dist)
        dst = xa.at[origin] if kind == 0 else kv.at[1, origin]
        return pltpu.make_async_remote_copy(
            src_ref=dst,
            dst_ref=dst,
            send_sem=send_sem.at[kind, way, dist - 1],
            recv_sem=recv_sem.at[kind, way, dist - 1],
            device_id=(sec, pos + 1 if way == 1 else pos - 1),
            device_id_type=MESH,
        )

    def start_own(kind):
        for way in range(2):
            @pl.when(sends(way, 1))
            def _():
                hop(kind, way, 1, True).start()

    start_own(0)

    state_copy = pltpu.make_async_remote_copy(
        src_ref=state_hbm.at[0],
        dst_ref=s_ref.at[0],
        send_sem=st_send,
        recv_sem=st_recv,
        device_id=(nxt, pos),
        device_id_type=MESH,
    )

    @pl.when(sec != last)
    def _():
        state_copy.start()

    small[0].wait()
    small[1].wait()
    plan = rows_ref[sec]
    shift = mods_ref[3 * plan + 0]
    scale = 1.0 + mods_ref[3 * plan + 1]
    gate = mods_ref[3 * plan + 2]

    def modulate(values):
        return (normalize(values.astype(F32)) * scale + shift).astype(BF16)

    modded = modulate(x_ref[0])
    for g in range(2):
        w_copies[g].wait()
        made = jnp.dot(modded, w_buf[g], preferred_element_type=F32).astype(BF16)
        kv[0, pos, :, g * width : (g + 1) * width] = made[:half]
        kv[1, pos, :, g * width : (g + 1) * width] = made[half:]
    start_own(1)
    w_copies[2].wait()
    queries = jnp.dot(modded, w_buf[2], preferred_element_type=F32)
    lane = lax.broadcasted_iota(jnp.int32, (local, lanes), 1)

    def spread(group, values):
        for pair in range(pairs):
            q_pair = values[:, pair * lanes : (pair + 1) * lanes]
            qs[group, pair, :local] = jnp.where(lane < head_size, q_pair, 0.0).astype(BF16)
            qs[group, pair, local:] = jnp.where(lane < head_size, 0.0, q_pair).astype(BF16)

    ends = ((0, 1), (n - 1, n - 2))
    at_end = jnp.logical_or(pos == 0, pos == n - 1)
    at_hub = jnp.logical_or(pos == 1, pos == n - 2)

    def query_copy(hub):
        return pltpu.make_async_remote_copy(
            src_ref=q_out,
            dst_ref=q_in,
            send_sem=q_send,
            recv_sem=q_recv,
            device_id=(sec, hub),
            device_id_type=MESH,
        )

    def mixed_copy(pair, end):
        return pltpu.make_async_remote_copy(
            src_ref=o_out.at[pair],
            dst_ref=o_in.at[pair],
            send_sem=o_send.at[pair],
            recv_sem=o_recv.at[pair],
            device_id=(sec, end),
            device_id_type=MESH,
        )

    @pl.when(at_end)
    def _():
        q_out[...] = queries.astype(BF16)

    for end, hub in ends:
        @pl.when(pos == end)
        def _():
            query_copy(hub).start()

    @pl.when(jnp.logical_not(at_end))
    def _():
        spread(0, queries)

    def take(kind, way, dist):
        @pl.when(gets(way, dist))
        def _():
            arrival(kind, way, dist).wait_recv()

        @pl.when(jnp.logical_and(gets(way, dist), sends(way, dist + 1)))
        def _():
            hop(kind, way, dist + 1, False).start()

    low_slot = lax.div(2 * pos, n)
    far_slot = (n - 1) * (1 - low_slot)

    def step(dist, carry):
        for way in range(2):
            take(0, way, dist)
        for way in range(2):
            @pl.when(gets(way, dist))
            def _():
                origin = source(way, dist)
                far = modulate(xa[origin])
                for g in range(2):
                    kv[0, origin, :, g * width : (g + 1) * width] = jnp.dot(
                        far, w_buf[g], preferred_element_type=F32
                    ).astype(BF16)

        for way in range(2):
            take(1, way, dist)

        return carry

    lax.fori_loop(1, n - 2, step, 0)

    upper = lax.broadcasted_iota(jnp.int32, (2 * local, 1), 0) < local

    def block(group, kind, pair):
        low = pair * lanes
        held = pl.ds(low_slot, n - 1) if kind == 0 else pl.ds(far_slot, 1)
        keys = kv[:, held, :, low : low + lanes].reshape(-1, lanes)
        values = kv[:, held, :, width + low : width + low + lanes].reshape(-1, lanes)
        factor = jnp.where(upper, mult_ref[0, 2 * pair], mult_ref[0, 2 * pair + 1])
        scores = lax.dot_general(
            qs[group, pair], keys, (((1,), (1,)), ((), ())), preferred_element_type=F32
        ) * (factor / math.sqrt(head_size))
        row_top = jnp.max(scores, axis=-1, keepdims=True)
        expd = jnp.exp(scores - row_top)
        row_sum = jnp.sum(expd, axis=-1, keepdims=True)
        mixed = jnp.dot(expd.astype(BF16), values, preferred_element_type=F32)
        return row_top, row_sum, mixed

    def first(group):
        for pair in range(pairs):
            row_top, row_sum, mixed = block(group, 0, pair)
            top[group, pair] = row_top
            total[group, pair] = row_sum
            acc[group, pair] = mixed

    def second(group, pair):
        row_top, row_sum, mixed = block(group, 1, pair)
        new_top = jnp.maximum(top[group, pair], row_top)
        before = jnp.exp(top[group, pair] - new_top)
        now = jnp.exp(row_top - new_top)
        row_sum = total[group, pair] * before + row_sum * now
        mixed = (acc[group, pair] * before + mixed * now) / row_sum
        return jnp.where(lane < head_size, mixed[:local], mixed[local:]).astype(BF16)

    @pl.when(jnp.logical_not(at_end))
    def _():
        first(0)

    @pl.when(at_hub)
    def _():
        query_copy(pos).wait_recv()
        spread(1, q_in[...].astype(F32))
        first(1)

    step(n - 2, 0)

    @pl.when(at_hub)
    def _():
        for group in (range(pairs // 2), range(pairs // 2, pairs)):
            for pair in group:
                o_out[pair] = second(1, pair)
            for end, hub in ends:
                @pl.when(pos == hub)
                def _():
                    for pair in group:
                        mixed_copy(pair, end).start()

    @pl.when(jnp.logical_not(at_end))
    def _():
        for pair in range(pairs):
            att[:, pair * lanes : (pair + 1) * lanes] = second(0, pair)

    @pl.when(at_end)
    def _():
        for pair in range(pairs):
            mixed_copy(pair, pos).wait_recv()
            att[:, pair * lanes : (pair + 1) * lanes] = o_in[pair]

    rest[0].wait()
    out_copies = []
    for c in range(chunks):
        span = slice(c * cols, (c + 1) * cols)
        branch = jnp.dot(att[...], wout_buf[:, span], preferred_element_type=F32)
        ybuf[c] = (x_ref[0, :, span].astype(F32) + gate[:, span] * branch).astype(BF16)
        copy = pltpu.make_async_remote_copy(
            src_ref=ybuf.at[c],
            dst_ref=h_ref.at[0, :, pl.ds(c * cols, cols)],
            send_sem=out_send.at[c],
            recv_sem=out_recv.at[c],
            device_id=(nxt, pos),
            device_id_type=MESH,
        )
        out_copies.append(copy)

        @pl.when(sec != last)
        def _():
            copy.start()

    for copy in rest[1:] + small[2:]:
        copy.wait()
    upd_copy = pltpu.make_async_remote_copy(
        src_ref=upd,
        dst_ref=s_ref.at[0],
        send_sem=st_send,
        recv_sem=st_recv,
        device_id=(nxt, pos),
        device_id_type=MESH,
    )

    @pl.when(sec == last)
    def _():
        stream = jnp.concatenate([ybuf[c] for c in range(chunks)], axis=1)
        normed = normalize(stream.astype(F32)).astype(BF16)
        predicted = jnp.dot(normed, read_buf[...], preferred_element_type=F32)
        upd[...] = (
            coef_ref[0, plan] * state_ref[0].astype(F32)
            + coef_ref[1, plan] * predicted
            + coef_ref[2, plan] * noise_ref[0].astype(F32)
        ).astype(BF16)
        upd_copy.start()

    state_copy.wait_recv()

    @pl.when(sec == 0)
    def _():
        member = ens_ref[pl.ds(slots_ref[last], 1), :]
        h_ref[0] = (
            jnp.dot(s_ref[0], lift_buf[...], preferred_element_type=F32) + member
        ).astype(BF16)

    @pl.when(sec != 0)
    def _():
        for copy in out_copies:
            copy.wait_recv()

    @pl.when(sec != last)
    def _():
        for copy in out_copies:
            copy.wait_send()

    state_copy.wait_send()

    def drain(dist, carry):
        for kind in range(2):
            for way in range(2):
                @pl.when(sends(way, dist))
                def _():
                    hop(kind, way, dist, False).wait_send()

        return carry

    lax.fori_loop(1, n, drain, 0)

    for end, hub in ends:
        @pl.when(pos == end)
        def _():
            query_copy(hub).wait_send()

        @pl.when(pos == hub)
        def _():
            for pair in range(pairs):
                mixed_copy(pair, end).wait_send()


def hub_kernel(
    n, sections, heads,
    rows_ref, slots_ref, mult_ref, coef_ref,
    x_hbm, state_hbm, noise_hbm, mods_hbm, ens_hbm,
    wqkv_ref, wout_ref, lift_ref, read_ref,
    h_ref, s_ref,
    w_buf, wout_buf, lift_buf, read_buf, xa, modded, keys, vext, qs, o_out, att, ybuf, upd,
    x_ref, state_ref, noise_ref, mods_ref, ens_ref,
    local_sem, x_send, x_recv, o_send, o_recv, y_send, y_recv, st_send, st_recv,
):
    sec = lax.axis_index("section")
    pos = lax.axis_index("tok")
    last = sections - 1
    nxt = lax.rem(sec + 1, sections)
    prev = lax.rem(sec + sections - 1, sections)
    local = x_hbm.shape[1]
    half = local // 2
    width = wout_ref.shape[1]
    model = x_hbm.shape[2]
    head_size = width // heads
    pairs = heads // 2
    lanes = 2 * head_size
    peers = n - 1
    side = peers * half

    odd = lax.rem(sec, 2)
    place_of = odd * pos + (1 - odd) * (n - 1 - pos)
    hub = odd * 1 + (1 - odd) * (n - 2)
    at_hub = place_of == 1
    slot = lax.rem(place_of + 2, n)

    def peer(index):
        where = (index + 2) % n
        return odd * where + (1 - odd) * (n - 1 - where)

    w_copy = pltpu.make_async_copy(wqkv_ref.at[0], w_buf, local_sem.at[0])
    wout_copy = pltpu.make_async_copy(wout_ref.at[0], wout_buf, local_sem.at[1])
    first = [
        pltpu.make_async_copy(x_hbm, x_ref, local_sem.at[2]),
        pltpu.make_async_copy(mods_hbm, mods_ref, local_sem.at[3]),
    ]
    late = [
        pltpu.make_async_copy(lift_ref, lift_buf, local_sem.at[4]),
        pltpu.make_async_copy(read_ref, read_buf, local_sem.at[5]),
        pltpu.make_async_copy(state_hbm, state_ref, local_sem.at[6]),
        pltpu.make_async_copy(noise_hbm, noise_ref, local_sem.at[7]),
        pltpu.make_async_copy(ens_hbm, ens_ref, local_sem.at[8]),
    ]
    barrier = pltpu.get_barrier_semaphore()

    def greet(device):
        pl.semaphore_signal(barrier, inc=1, device_id=device, device_id_type=MESH)

    @pl.when(at_hub)
    def _():
        for index in range(peers):
            greet((sec, peer(index)))

    @pl.when(jnp.logical_not(at_hub))
    def _():
        greet((sec, hub))

    greet((nxt, pos))
    greet((prev, pos))
    for copy in first:
        copy.start()

    @pl.when(at_hub)
    def _():
        w_copy.start()

    for copy in [wout_copy] + late:
        copy.start()

    def x_copy(slot_at, piece):
        return pltpu.make_async_remote_copy(
            src_ref=modded.at[pl.ds(piece * half, half), :],
            dst_ref=xa.at[piece, slot_at],
            send_sem=x_send.at[piece],
            recv_sem=x_recv.at[piece, slot_at],
            device_id=(sec, hub),
            device_id_type=MESH,
        )

    def o_copy(piece, index, part):
        cols = pl.ds(part * (width // 2), width // 2)
        return pltpu.make_async_remote_copy(
            src_ref=o_out.at[piece, index, :, cols],
            dst_ref=att.at[pl.ds(piece * half, half), cols],
            send_sem=o_send.at[piece, index, part],
            recv_sem=o_recv.at[piece, part],
            device_id=(sec, peer(index)),
            device_id_type=MESH,
        )

    def y_copy(piece):
        return pltpu.make_async_remote_copy(
            src_ref=ybuf.at[pl.ds(piece * half, half), :],
            dst_ref=h_ref.at[0, pl.ds(piece * half, half), :],
            send_sem=y_send.at[piece],
            recv_sem=y_recv.at[piece],
            device_id=(nxt, pos),
            device_id_type=MESH,
        )

    state_copy = pltpu.make_async_remote_copy(
        src_ref=state_hbm.at[0],
        dst_ref=s_ref.at[0],
        send_sem=st_send,
        recv_sem=st_recv,
        device_id=(nxt, pos),
        device_id_type=MESH,
    )

    for copy in first:
        copy.wait()
    plan = rows_ref[sec]
    shift = mods_ref[3 * plan + 0]
    scale = 1.0 + mods_ref[3 * plan + 1]
    gate = mods_ref[3 * plan + 2]
    modded[...] = (normalize(x_ref[0].astype(F32)) * scale + shift).astype(BF16)

    @pl.when(jnp.logical_not(at_hub))
    def _():
        pl.semaphore_wait(barrier, 3)
        for piece in range(2):
            x_copy(slot, piece).start()

    @pl.when(at_hub)
    def _():
        pl.semaphore_wait(barrier, 2 + peers)

    @pl.when(sec != last)
    def _():
        state_copy.start()

    def branch_rows(piece, mixed):
        rows = slice(piece * half, (piece + 1) * half)
        branch = jnp.dot(mixed, wout_buf[...], preferred_element_type=F32)
        ybuf[rows, :] = (x_ref[0, rows, :].astype(F32) + gate * branch).astype(BF16)

        @pl.when(sec != last)
        def _():
            y_copy(piece).start()

    def project(rows, values):
        made = jnp.dot(values, w_buf[...], preferred_element_type=F32).astype(BF16)
        qs[rows, :] = made[:, :width]
        keys[rows, :] = made[:, width : 2 * width]
        for pair in range(pairs):
            low = 2 * width + pair * lanes
            vext[pair, rows, :lanes] = made[:, low : low + lanes]

    log2e = 1.0 / math.log(2.0)

    def attend(start, count, pair):
        low = pair * lanes
        lane = lax.broadcasted_iota(jnp.int32, (count, lanes), 1)
        query = qs[start : start + count, low : low + lanes]
        zero = jnp.zeros_like(query)
        stacked = jnp.concatenate(
            [jnp.where(lane < head_size, query, zero), jnp.where(lane < head_size, zero, query)],
            axis=0,
        )
        scores = lax.dot_general(
            stacked, keys[:, low : low + lanes], (((1,), (1,)), ((), ())), preferred_element_type=F32
        )
        expd = []
        for one in range(2):
            part = scores[one * count : (one + 1) * count]
            factor = mult_ref[0, 2 * pair + one] * (log2e / math.sqrt(head_size))
            top = jnp.max(part, axis=-1, keepdims=True)
            weights = jnp.exp2(part * factor - top * factor)
            expd.append(weights.astype(BF16))
        mixed = jnp.dot(
            jnp.concatenate(expd, axis=0),
            vext[pair],
            preferred_element_type=F32,
        )
        weighted = jnp.where(lane < head_size, mixed[:count, :lanes], mixed[count:, :lanes])
        row_sum = jnp.where(lane < head_size, mixed[:count, lanes:], mixed[count:, lanes:])
        return (weighted / row_sum).astype(BF16)

    @pl.when(at_hub)
    def _():
        vext[:, :, lanes:] = jnp.ones((pairs, n * local, lanes), BF16)
        w_copy.wait()
        project(slice(0, local), modded[...])
        for piece in range(2):
            for index in range(peers):
                x_copy(index, piece).wait_recv()
            start = local + piece * side
            project(slice(start, start + side), xa[piece].reshape(side, model))
        for piece in range(2):
            for part in range(2):
                for pair in range(part * pairs // 2, (part + 1) * pairs // 2):
                    mixed = attend(local + piece * side, side, pair)
                    for index in range(peers):
                        o_out[piece, index, :, pair * lanes : (pair + 1) * lanes] = mixed[
                            index * half : (index + 1) * half
                        ]
                for index in (1, 0, 2):
                    o_copy(piece, index, part).start()
        for pair in range(pairs):
            att[:, pair * lanes : (pair + 1) * lanes] = attend(0, local, pair)

    wout_copy.wait()
    for piece in range(2):
        @pl.when(jnp.logical_not(at_hub))
        def _():
            for part in range(2):
                o_copy(piece, 0, part).wait_recv()

        branch_rows(piece, att[piece * half : (piece + 1) * half, :])

    for copy in late:
        copy.wait()
    upd_copy = pltpu.make_async_remote_copy(
        src_ref=upd,
        dst_ref=s_ref.at[0],
        send_sem=st_send,
        recv_sem=st_recv,
        device_id=(nxt, pos),
        device_id_type=MESH,
    )

    @pl.when(sec == last)
    def _():
        normed = normalize(ybuf[...].astype(F32)).astype(BF16)
        predicted = jnp.dot(normed, read_buf[...], preferred_element_type=F32)
        upd[...] = (
            coef_ref[0, plan] * state_ref[0].astype(F32)
            + coef_ref[1, plan] * predicted
            + coef_ref[2, plan] * noise_ref[0].astype(F32)
        ).astype(BF16)
        upd_copy.start()

    state_copy.wait_recv()

    @pl.when(sec == 0)
    def _():
        member = ens_ref[pl.ds(slots_ref[last], 1), :]
        h_ref[0] = (
            jnp.dot(s_ref[0], lift_buf[...], preferred_element_type=F32) + member
        ).astype(BF16)

    @pl.when(sec != 0)
    def _():
        for piece in range(2):
            y_copy(piece).wait_recv()

    @pl.when(sec != last)
    def _():
        for piece in range(2):
            y_copy(piece).wait_send()

    state_copy.wait_send()

    @pl.when(at_hub)
    def _():
        for piece in range(2):
            for part in range(2):
                for index in range(peers):
                    o_copy(piece, index, part).wait_send()

    @pl.when(jnp.logical_not(at_hub))
    def _():
        for piece in range(2):
            x_copy(slot, piece).wait_send()


def place(h_in, s_in, h_out, s_out, sem):
    copies = [
        pltpu.make_async_copy(h_in, h_out, sem.at[0]),
        pltpu.make_async_copy(s_in, s_out, sem.at[1]),
    ]
    for copy in copies:
        copy.start()
    for copy in copies:
        copy.wait()


def body(
    n, sections,
    carried_activations,
    corrupted_field,
    gaussian_perturbation,
    timeline_entry_number,
    ensemble_slots,
    attention_entry_matrices,
    attention_exit_matrix,
    adaptive_norm_terms,
    score_multiplier,
    lifting_matrix,
    readout_matrix,
    ensemble_vectors,
    denoiser_coefficients,
):
    _, local, model = carried_activations.shape
    channels = corrupted_field.shape[2]
    width = attention_exit_matrix.shape[1]
    heads = score_multiplier.shape[1]
    half = local // 2
    pairs = heads // 2
    lanes = 2 * (width // heads)
    chunks = 3
    terms = adaptive_norm_terms.reshape(-1, 1, model)
    smem = pl.BlockSpec(memory_space=pltpu.SMEM)
    vmem = pl.BlockSpec(memory_space=pltpu.VMEM)
    hbm = pl.BlockSpec(memory_space=pl.ANY)
    def dma(*shape):
        return pltpu.SemaphoreType.DMA(shape)

    staged = [
        pltpu.VMEM(carried_activations.shape, BF16),
        pltpu.VMEM(corrupted_field.shape, BF16),
        pltpu.VMEM(gaussian_perturbation.shape, BF16),
        pltpu.VMEM(terms.shape, F32),
        pltpu.VMEM(ensemble_vectors.shape, F32),
    ]
    if n == 4 and sections % 2 == 0 and heads % 4 == 0 and local % 32 == 0:
        run = functools.partial(hub_kernel, n, sections, heads)
        scratch = [
            pltpu.VMEM((model, 3 * width), BF16),
            pltpu.VMEM((width, model), BF16),
            pltpu.VMEM(lifting_matrix.shape, BF16),
            pltpu.VMEM(readout_matrix.shape, BF16),
            pltpu.VMEM((2, n - 1, half, model), BF16),
            pltpu.VMEM((local, model), BF16),
            pltpu.VMEM((n * local, width), BF16),
            pltpu.VMEM((pairs, n * local, 2 * lanes), BF16),
            pltpu.VMEM((n * local, width), BF16),
            pltpu.VMEM((2, n - 1, half, width), BF16),
            pltpu.VMEM((local, width), BF16),
            pltpu.VMEM((local, model), BF16),
            pltpu.VMEM((local, channels), BF16),
            *staged,
            dma(9), dma(2), dma(2, n - 1), dma(2, n - 1, 2), dma(2, 2), dma(2), dma(2),
            pltpu.SemaphoreType.DMA,
            pltpu.SemaphoreType.DMA,
        ]
    else:
        run = functools.partial(line_kernel, n, sections, heads, chunks)
        scratch = [
                pltpu.VMEM((3, model, width), BF16),
                pltpu.VMEM((width, model), BF16),
                pltpu.VMEM(lifting_matrix.shape, BF16),
                pltpu.VMEM(readout_matrix.shape, BF16),
                pltpu.VMEM((n, half, model), BF16),
                pltpu.VMEM((2, n, half, 2 * width), BF16),
                pltpu.VMEM((2, pairs, 2 * local, lanes), BF16),
                pltpu.VMEM((2, pairs, 2 * local, lanes), F32),
                pltpu.VMEM((2, pairs, 2 * local, 1), F32),
                pltpu.VMEM((2, pairs, 2 * local, 1), F32),
                pltpu.VMEM((local, width), BF16),
                pltpu.VMEM((chunks, local, model // chunks), BF16),
                pltpu.VMEM((local, channels), BF16),
                pltpu.VMEM((local, width), BF16),
                pltpu.VMEM((local, width), BF16),
                pltpu.VMEM((pairs, local, lanes), BF16),
                pltpu.VMEM((pairs, local, lanes), BF16),
                pltpu.VMEM(carried_activations.shape, BF16),
                pltpu.VMEM(corrupted_field.shape, BF16),
                pltpu.VMEM(gaussian_perturbation.shape, BF16),
                pltpu.VMEM(terms.shape, F32),
                pltpu.VMEM(ensemble_vectors.shape, F32),
                pltpu.SemaphoreType.DMA((11,)),
                pltpu.SemaphoreType.DMA((2, 2, n - 1)),
                pltpu.SemaphoreType.DMA((2, 2, n - 1)),
                pltpu.SemaphoreType.DMA((chunks,)),
                pltpu.SemaphoreType.DMA((chunks,)),
                pltpu.SemaphoreType.DMA,
                pltpu.SemaphoreType.DMA,
                pltpu.SemaphoreType.DMA,
                pltpu.SemaphoreType.DMA,
                pltpu.SemaphoreType.DMA((pairs,)),
                pltpu.SemaphoreType.DMA((pairs,)),
        ]
    stream, field = pl.pallas_call(
        run,
        out_shape=(
            pltpu.VMEM(carried_activations.shape, BF16),
            pltpu.VMEM(corrupted_field.shape, BF16),
        ),
        in_specs=[smem] * 4 + [hbm] * 9,
        out_specs=(vmem, vmem),
        scratch_shapes=scratch,
        compiler_params=pltpu.CompilerParams(
            collective_id=0, has_side_effects=True, vmem_limit_bytes=60 * 1024 * 1024
        ),
        name="denoise_pass",
    )(
        timeline_entry_number,
        ensemble_slots,
        score_multiplier,
        denoiser_coefficients.T,
        carried_activations,
        corrupted_field,
        gaussian_perturbation,
        terms,
        ensemble_vectors,
        attention_entry_matrices,
        attention_exit_matrix,
        lifting_matrix,
        readout_matrix,
    )
    return pl.pallas_call(
        place,
        out_shape=(
            jax.ShapeDtypeStruct(stream.shape, BF16),
            jax.ShapeDtypeStruct(field.shape, BF16),
        ),
        in_specs=[vmem, vmem],
        out_specs=(hbm, hbm),
        scratch_shapes=[pltpu.SemaphoreType.DMA((2,))],
        name="place_results",
    )(
        pltpu.with_memory_space_constraint(stream, pltpu.VMEM),
        pltpu.with_memory_space_constraint(field, pltpu.VMEM),
    )


def solution(mesh):
    placed = (
        P("section", "tok", None),
        P("section", "tok", None),
        P(None, "tok", None),
        P(),
        P(),
        P("section", None, None),
        P("section", None, None),
        P("section", None, None, None),
        P("section", None),
        P(),
        P(),
        P(),
        P(),
    )
    return jax.shard_map(
        functools.partial(body, mesh.shape["tok"], mesh.shape["section"]),
        mesh=mesh,
        in_specs=placed,
        out_specs=(P("section", "tok", None), P("section", "tok", None)),
        check_vma=False,
    )
```

```python
import functools
import math

import jax
import jax.numpy as jnp
from jax import lax
from jax.experimental import pallas as pl
from jax.experimental.pallas import tpu as pltpu
from jax.sharding import PartitionSpec as P

MESH = pl.DeviceIdType.MESH
F32 = jnp.float32
BF16 = jnp.bfloat16


def normalize(values):
    row_mean = jnp.mean(values, axis=-1, keepdims=True)
    centred = values - row_mean
    row_var = jnp.mean(centred * centred, axis=-1, keepdims=True)
    return centred * lax.rsqrt(row_var + 1e-06)


def line_kernel(
    n, sections, heads, chunks,
    rows_ref, slots_ref, mult_ref, coef_ref,
    x_hbm, state_hbm, noise_hbm, mods_hbm, ens_hbm,
    wqkv_ref, wout_ref, lift_ref, read_ref,
    h_ref, s_ref,
    w_buf, wout_buf, lift_buf, read_buf, xa, kv, qs, acc, top, total, att, ybuf, upd, q_out, q_in, o_out, o_in,
    x_ref, state_ref, noise_ref, mods_ref, ens_ref,
    local_sem, send_sem, recv_sem, out_send, out_recv, st_send, st_recv,
    q_send, q_recv, o_send, o_recv,
):
    sec = lax.axis_index("section")
    pos = lax.axis_index("tok")
    last = sections - 1
    nxt = lax.rem(sec + 1, sections)
    prev = lax.rem(sec + sections - 1, sections)
    local = x_hbm.shape[1]
    half = local // 2
    width = wout_ref.shape[1]
    model = x_hbm.shape[2]
    head_size = width // heads
    pairs = heads // 2
    lanes = 2 * head_size
    cols = model // chunks

    starts = (width, 2 * width, 0)
    w_copies = [
        pltpu.make_async_copy(
            wqkv_ref.at[0, :, pl.ds(starts[g], width)], w_buf.at[g], local_sem.at[g]
        )
        for g in range(3)
    ]
    rest = [
        pltpu.make_async_copy(wout_ref.at[0], wout_buf, local_sem.at[3]),
        pltpu.make_async_copy(lift_ref, lift_buf, local_sem.at[4]),
        pltpu.make_async_copy(read_ref, read_buf, local_sem.at[5]),
    ]
    small = [
        pltpu.make_async_copy(source_ref, target_ref, local_sem.at[6 + i])
        for i, (source_ref, target_ref) in enumerate(
            (
                (x_hbm, x_ref),
                (mods_hbm, mods_ref),
                (state_hbm, state_ref),
                (noise_hbm, noise_ref),
                (ens_hbm, ens_ref),
            )
        )
    ]
    for copy in small + w_copies + rest:
        copy.start()

    barrier = pltpu.get_barrier_semaphore()
    has_up = pos + 1 < n
    has_down = pos > 0

    @pl.when(has_up)
    def _():
        pl.semaphore_signal(barrier, inc=1, device_id=(sec, pos + 1), device_id_type=MESH)

    @pl.when(has_down)
    def _():
        pl.semaphore_signal(barrier, inc=1, device_id=(sec, pos - 1), device_id_type=MESH)

    pl.semaphore_signal(barrier, inc=1, device_id=(nxt, pos), device_id_type=MESH)
    pl.semaphore_signal(barrier, inc=1, device_id=(prev, pos), device_id_type=MESH)
    pl.semaphore_wait(barrier, 2 + has_up.astype(jnp.int32) + has_down.astype(jnp.int32))

    def hop(kind, way, dist, own):
        origin = pos - (dist - 1) if way == 0 else pos + (dist - 1)
        target = pos + 1 if way == 0 else pos - 1
        if kind == 0:
            dst = xa.at[origin]
            src = x_hbm.at[0, pl.ds(0, half), :] if own else dst
        else:
            dst = kv.at[1, origin]
            src = dst
        return pltpu.make_async_remote_copy(
            src_ref=src,
            dst_ref=dst,
            send_sem=send_sem.at[kind, way, dist - 1],
            recv_sem=recv_sem.at[kind, way, dist - 1],
            device_id=(sec, target),
            device_id_type=MESH,
        )

    def sends(way, dist):
        if way == 0:
            return jnp.logical_and(pos + 2 < n, pos - (dist - 1) >= 0)
        return jnp.logical_and(pos > 1, pos + (dist - 1) < n)

    def gets(way, dist):
        if way == 0:
            return jnp.logical_and(pos + 1 < n, pos - dist >= 0)
        return jnp.logical_and(pos > 0, pos + dist < n)

    def source(way, dist):
        return pos - dist if way == 0 else pos + dist

    def arrival(kind, way, dist):
        origin = source(way, dist)
        dst = xa.at[origin] if kind == 0 else kv.at[1, origin]
        return pltpu.make_async_remote_copy(
            src_ref=dst,
            dst_ref=dst,
            send_sem=send_sem.at[kind, way, dist - 1],
            recv_sem=recv_sem.at[kind, way, dist - 1],
            device_id=(sec, pos + 1 if way == 1 else pos - 1),
            device_id_type=MESH,
        )

    def start_own(kind):
        for way in range(2):
            @pl.when(sends(way, 1))
            def _():
                hop(kind, way, 1, True).start()

    start_own(0)

    state_copy = pltpu.make_async_remote_copy(
        src_ref=state_hbm.at[0],
        dst_ref=s_ref.at[0],
        send_sem=st_send,
        recv_sem=st_recv,
        device_id=(nxt, pos),
        device_id_type=MESH,
    )

    @pl.when(sec != last)
    def _():
        state_copy.start()

    small[0].wait()
    small[1].wait()
    plan = rows_ref[sec]
    shift = mods_ref[3 * plan + 0]
    scale = 1.0 + mods_ref[3 * plan + 1]
    gate = mods_ref[3 * plan + 2]

    def modulate(values):
        return (normalize(values.astype(F32)) * scale + shift).astype(BF16)

    modded = modulate(x_ref[0])
    for g in range(2):
        w_copies[g].wait()
        made = jnp.dot(modded, w_buf[g], preferred_element_type=F32).astype(BF16)
        kv[0, pos, :, g * width : (g + 1) * width] = made[:half]
        kv[1, pos, :, g * width : (g + 1) * width] = made[half:]
    start_own(1)
    w_copies[2].wait()
    queries = jnp.dot(modded, w_buf[2], preferred_element_type=F32)
    lane = lax.broadcasted_iota(jnp.int32, (local, lanes), 1)

    def spread(group, values):
        for pair in range(pairs):
            q_pair = values[:, pair * lanes : (pair + 1) * lanes]
            qs[group, pair, :local] = jnp.where(lane < head_size, q_pair, 0.0).astype(BF16)
            qs[group, pair, local:] = jnp.where(lane < head_size, 0.0, q_pair).astype(BF16)

    ends = ((0, 1), (n - 1, n - 2))
    at_end = jnp.logical_or(pos == 0, pos == n - 1)
    at_hub = jnp.logical_or(pos == 1, pos == n - 2)

    def query_copy(hub):
        return pltpu.make_async_remote_copy(
            src_ref=q_out,
            dst_ref=q_in,
            send_sem=q_send,
            recv_sem=q_recv,
            device_id=(sec, hub),
            device_id_type=MESH,
        )

    def mixed_copy(pair, end):
        return pltpu.make_async_remote_copy(
            src_ref=o_out.at[pair],
            dst_ref=o_in.at[pair],
            send_sem=o_send.at[pair],
            recv_sem=o_recv.at[pair],
            device_id=(sec, end),
            device_id_type=MESH,
        )

    @pl.when(at_end)
    def _():
        q_out[...] = queries.astype(BF16)

    for end, hub in ends:
        @pl.when(pos == end)
        def _():
            query_copy(hub).start()

    @pl.when(jnp.logical_not(at_end))
    def _():
        spread(0, queries)

    def take(kind, way, dist):
        @pl.when(gets(way, dist))
        def _():
            arrival(kind, way, dist).wait_recv()

        @pl.when(jnp.logical_and(gets(way, dist), sends(way, dist + 1)))
        def _():
            hop(kind, way, dist + 1, False).start()

    low_slot = lax.div(2 * pos, n)
    far_slot = (n - 1) * (1 - low_slot)

    def step(dist, carry):
        for way in range(2):
            take(0, way, dist)
        for way in range(2):
            @pl.when(gets(way, dist))
            def _():
                origin = source(way, dist)
                far = modulate(xa[origin])
                for g in range(2):
                    kv[0, origin, :, g * width : (g + 1) * width] = jnp.dot(
                        far, w_buf[g], preferred_element_type=F32
                    ).astype(BF16)

        for way in range(2):
            take(1, way, dist)

        return carry

    lax.fori_loop(1, n - 2, step, 0)

    upper = lax.broadcasted_iota(jnp.int32, (2 * local, 1), 0) < local

    def block(group, kind, pair):
        low = pair * lanes
        held = pl.ds(low_slot, n - 1) if kind == 0 else pl.ds(far_slot, 1)
        keys = kv[:, held, :, low : low + lanes].reshape(-1, lanes)
        values = kv[:, held, :, width + low : width + low + lanes].reshape(-1, lanes)
        factor = jnp.where(upper, mult_ref[0, 2 * pair], mult_ref[0, 2 * pair + 1])
        scores = lax.dot_general(
            qs[group, pair], keys, (((1,), (1,)), ((), ())), preferred_element_type=F32
        ) * (factor / math.sqrt(head_size))
        row_top = jnp.max(scores, axis=-1, keepdims=True)
        expd = jnp.exp(scores - row_top)
        row_sum = jnp.sum(expd, axis=-1, keepdims=True)
        mixed = jnp.dot(expd.astype(BF16), values, preferred_element_type=F32)
        return row_top, row_sum, mixed

    def first(group):
        for pair in range(pairs):
            row_top, row_sum, mixed = block(group, 0, pair)
            top[group, pair] = row_top
            total[group, pair] = row_sum
            acc[group, pair] = mixed

    def second(group, pair):
        row_top, row_sum, mixed = block(group, 1, pair)
        new_top = jnp.maximum(top[group, pair], row_top)
        before = jnp.exp(top[group, pair] - new_top)
        now = jnp.exp(row_top - new_top)
        row_sum = total[group, pair] * before + row_sum * now
        mixed = (acc[group, pair] * before + mixed * now) / row_sum
        return jnp.where(lane < head_size, mixed[:local], mixed[local:]).astype(BF16)

    @pl.when(jnp.logical_not(at_end))
    def _():
        first(0)

    @pl.when(at_hub)
    def _():
        query_copy(pos).wait_recv()
        spread(1, q_in[...].astype(F32))
        first(1)

    step(n - 2, 0)

    @pl.when(at_hub)
    def _():
        for group in (range(pairs // 2), range(pairs // 2, pairs)):
            for pair in group:
                o_out[pair] = second(1, pair)
            for end, hub in ends:
                @pl.when(pos == hub)
                def _():
                    for pair in group:
                        mixed_copy(pair, end).start()

    @pl.when(jnp.logical_not(at_end))
    def _():
        for pair in range(pairs):
            att[:, pair * lanes : (pair + 1) * lanes] = second(0, pair)

    @pl.when(at_end)
    def _():
        for pair in range(pairs):
            mixed_copy(pair, pos).wait_recv()
            att[:, pair * lanes : (pair + 1) * lanes] = o_in[pair]

    rest[0].wait()
    out_copies = []
    for c in range(chunks):
        span = slice(c * cols, (c + 1) * cols)
        branch = jnp.dot(att[...], wout_buf[:, span], preferred_element_type=F32)
        ybuf[c] = (x_ref[0, :, span].astype(F32) + gate[:, span] * branch).astype(BF16)
        copy = pltpu.make_async_remote_copy(
            src_ref=ybuf.at[c],
            dst_ref=h_ref.at[0, :, pl.ds(c * cols, cols)],
            send_sem=out_send.at[c],
            recv_sem=out_recv.at[c],
            device_id=(nxt, pos),
            device_id_type=MESH,
        )
        out_copies.append(copy)

        @pl.when(sec != last)
        def _():
            copy.start()

    for copy in rest[1:] + small[2:]:
        copy.wait()
    upd_copy = pltpu.make_async_remote_copy(
        src_ref=upd,
        dst_ref=s_ref.at[0],
        send_sem=st_send,
        recv_sem=st_recv,
        device_id=(nxt, pos),
        device_id_type=MESH,
    )

    @pl.when(sec == last)
    def _():
        stream = jnp.concatenate([ybuf[c] for c in range(chunks)], axis=1)
        normed = normalize(stream.astype(F32)).astype(BF16)
        predicted = jnp.dot(normed, read_buf[...], preferred_element_type=F32)
        upd[...] = (
            coef_ref[0, plan] * state_ref[0].astype(F32)
            + coef_ref[1, plan] * predicted
            + coef_ref[2, plan] * noise_ref[0].astype(F32)
        ).astype(BF16)
        upd_copy.start()

    state_copy.wait_recv()

    @pl.when(sec == 0)
    def _():
        member = ens_ref[pl.ds(slots_ref[last], 1), :]
        h_ref[0] = (
            jnp.dot(s_ref[0], lift_buf[...], preferred_element_type=F32) + member
        ).astype(BF16)

    @pl.when(sec != 0)
    def _():
        for copy in out_copies:
            copy.wait_recv()

    @pl.when(sec != last)
    def _():
        for copy in out_copies:
            copy.wait_send()

    state_copy.wait_send()

    def drain(dist, carry):
        for kind in range(2):
            for way in range(2):
                @pl.when(sends(way, dist))
                def _():
                    hop(kind, way, dist, False).wait_send()

        return carry

    lax.fori_loop(1, n, drain, 0)

    for end, hub in ends:
        @pl.when(pos == end)
        def _():
            query_copy(hub).wait_send()

        @pl.when(pos == hub)
        def _():
            for pair in range(pairs):
                mixed_copy(pair, end).wait_send()


def hub_kernel(
    n, sections, heads,
    rows_hbm, slots_hbm, mult_hbm, coef_hbm,
    x_hbm, state_hbm, noise_hbm, mods_hbm, ens_hbm,
    wqkv_ref, wout_ref, lift_ref, read_ref,
    h_ref, s_ref,
    w_buf, wout_buf, lift_buf, read_buf, xa, modded, keys, vext, qs, o_out, att, ybuf, upd,
    x_ref, state_ref, noise_ref, mods_ref, ens_ref,
    rows_ref, slots_ref, mult_ref, coef_ref,
    local_sem, x_send, x_recv, o_send, o_recv, y_send, y_recv, st_send, st_recv,
):
    sec = lax.axis_index("section")
    pos = lax.axis_index("tok")
    last = sections - 1
    nxt = lax.rem(sec + 1, sections)
    prev = lax.rem(sec + sections - 1, sections)
    local = x_hbm.shape[1]
    half = local // 2
    width = wout_ref.shape[1]
    model = x_hbm.shape[2]
    head_size = width // heads
    pairs = heads // 2
    lanes = 2 * head_size
    peers = n - 1
    side = peers * half

    odd = lax.rem(sec, 2)
    place_of = odd * pos + (1 - odd) * (n - 1 - pos)
    hub = odd * 1 + (1 - odd) * (n - 2)
    at_hub = place_of == 1
    slot = lax.rem(place_of + 2, n)

    def peer(index):
        where = (index + 2) % n
        return odd * where + (1 - odd) * (n - 1 - where)

    w_copy = pltpu.make_async_copy(wqkv_ref.at[0], w_buf, local_sem.at[0])
    wout_copy = pltpu.make_async_copy(wout_ref.at[0], wout_buf, local_sem.at[1])
    first = [
        pltpu.make_async_copy(x_hbm, x_ref, local_sem.at[2]),
        pltpu.make_async_copy(mods_hbm, mods_ref, local_sem.at[3]),
        pltpu.make_async_copy(rows_hbm, rows_ref, local_sem.at[9]),
        pltpu.make_async_copy(mult_hbm, mult_ref, local_sem.at[10]),
    ]
    late = [
        pltpu.make_async_copy(lift_ref, lift_buf, local_sem.at[4]),
        pltpu.make_async_copy(read_ref, read_buf, local_sem.at[5]),
        pltpu.make_async_copy(state_hbm, state_ref, local_sem.at[6]),
        pltpu.make_async_copy(noise_hbm, noise_ref, local_sem.at[7]),
        pltpu.make_async_copy(ens_hbm, ens_ref, local_sem.at[8]),
        pltpu.make_async_copy(slots_hbm, slots_ref, local_sem.at[11]),
        pltpu.make_async_copy(coef_hbm, coef_ref, local_sem.at[12]),
    ]
    barrier = pltpu.get_barrier_semaphore()

    def greet(device):
        pl.semaphore_signal(barrier, inc=1, device_id=device, device_id_type=MESH)

    @pl.when(at_hub)
    def _():
        for index in range(peers):
            greet((sec, peer(index)))

    @pl.when(jnp.logical_not(at_hub))
    def _():
        greet((sec, hub))

    greet((nxt, pos))
    greet((prev, pos))
    for copy in first:
        copy.start()

    @pl.when(at_hub)
    def _():
        w_copy.start()

    for copy in [wout_copy] + late:
        copy.start()

    def x_copy(slot_at, piece):
        return pltpu.make_async_remote_copy(
            src_ref=modded.at[pl.ds(piece * half, half), :],
            dst_ref=xa.at[piece, slot_at],
            send_sem=x_send.at[piece],
            recv_sem=x_recv.at[piece, slot_at],
            device_id=(sec, hub),
            device_id_type=MESH,
        )

    def o_copy(piece, index, part):
        cols = pl.ds(part * (width // 2), width // 2)
        return pltpu.make_async_remote_copy(
            src_ref=o_out.at[piece, index, :, cols],
            dst_ref=att.at[pl.ds(piece * half, half), cols],
            send_sem=o_send.at[piece, index, part],
            recv_sem=o_recv.at[piece, part],
            device_id=(sec, peer(index)),
            device_id_type=MESH,
        )

    def y_copy(piece):
        return pltpu.make_async_remote_copy(
            src_ref=ybuf.at[pl.ds(piece * half, half), :],
            dst_ref=h_ref.at[0, pl.ds(piece * half, half), :],
            send_sem=y_send.at[piece],
            recv_sem=y_recv.at[piece],
            device_id=(nxt, pos),
            device_id_type=MESH,
        )

    state_copy = pltpu.make_async_remote_copy(
        src_ref=state_hbm.at[0],
        dst_ref=s_ref.at[0],
        send_sem=st_send,
        recv_sem=st_recv,
        device_id=(nxt, pos),
        device_id_type=MESH,
    )

    for copy in first:
        copy.wait()
    plan = rows_ref[sec]
    shift = mods_ref[3 * plan + 0]
    scale = 1.0 + mods_ref[3 * plan + 1]
    gate = mods_ref[3 * plan + 2]
    modded[...] = (normalize(x_ref[0].astype(F32)) * scale + shift).astype(BF16)

    @pl.when(jnp.logical_not(at_hub))
    def _():
        pl.semaphore_wait(barrier, 3)
        for piece in range(2):
            x_copy(slot, piece).start()

    @pl.when(at_hub)
    def _():
        pl.semaphore_wait(barrier, 2 + peers)

    @pl.when(sec != last)
    def _():
        state_copy.start()

    def branch_rows(piece, mixed):
        rows = slice(piece * half, (piece + 1) * half)
        branch = jnp.dot(mixed, wout_buf[...], preferred_element_type=F32)
        ybuf[rows, :] = (x_ref[0, rows, :].astype(F32) + gate * branch).astype(BF16)

        @pl.when(sec != last)
        def _():
            y_copy(piece).start()

    def project(rows, values):
        made = jnp.dot(values, w_buf[...], preferred_element_type=F32).astype(BF16)
        qs[rows, :] = made[:, :width]
        keys[rows, :] = made[:, width : 2 * width]
        for pair in range(pairs):
            low = 2 * width + pair * lanes
            vext[pair, rows, :lanes] = made[:, low : low + lanes]

    log2e = 1.0 / math.log(2.0)

    def attend(start, count, pair):
        low = pair * lanes
        lane = lax.broadcasted_iota(jnp.int32, (count, lanes), 1)
        query = qs[start : start + count, low : low + lanes]
        zero = jnp.zeros_like(query)
        stacked = jnp.concatenate(
            [jnp.where(lane < head_size, query, zero), jnp.where(lane < head_size, zero, query)],
            axis=0,
        )
        scores = lax.dot_general(
            stacked, keys[:, low : low + lanes], (((1,), (1,)), ((), ())), preferred_element_type=F32
        )
        expd = []
        for one in range(2):
            part = scores[one * count : (one + 1) * count]
            factor = mult_ref[0, 2 * pair + one] * (log2e / math.sqrt(head_size))
            top = jnp.max(part, axis=-1, keepdims=True)
            weights = jnp.exp2(part * factor - top * factor)
            expd.append(weights.astype(BF16))
        mixed = jnp.dot(
            jnp.concatenate(expd, axis=0),
            vext[pair],
            preferred_element_type=F32,
        )
        weighted = jnp.where(lane < head_size, mixed[:count, :lanes], mixed[count:, :lanes])
        row_sum = jnp.where(lane < head_size, mixed[:count, lanes:], mixed[count:, lanes:])
        return (weighted / row_sum).astype(BF16)

    @pl.when(at_hub)
    def _():
        vext[:, :, lanes:] = jnp.ones((pairs, n * local, lanes), BF16)
        w_copy.wait()
        project(slice(0, local), modded[...])
        for piece in range(2):
            for index in range(peers):
                x_copy(index, piece).wait_recv()
            start = local + piece * side
            project(slice(start, start + side), xa[piece].reshape(side, model))
        for piece in range(2):
            for part in range(2):
                for pair in range(part * pairs // 2, (part + 1) * pairs // 2):
                    mixed = attend(local + piece * side, side, pair)
                    for index in range(peers):
                        o_out[piece, index, :, pair * lanes : (pair + 1) * lanes] = mixed[
                            index * half : (index + 1) * half
                        ]
                for index in (1, 0, 2):
                    o_copy(piece, index, part).start()
        for pair in range(pairs):
            att[:, pair * lanes : (pair + 1) * lanes] = attend(0, local, pair)

    wout_copy.wait()
    for piece in range(2):
        @pl.when(jnp.logical_not(at_hub))
        def _():
            for part in range(2):
                o_copy(piece, 0, part).wait_recv()

        branch_rows(piece, att[piece * half : (piece + 1) * half, :])

    for copy in late:
        copy.wait()
    upd_copy = pltpu.make_async_remote_copy(
        src_ref=upd,
        dst_ref=s_ref.at[0],
        send_sem=st_send,
        recv_sem=st_recv,
        device_id=(nxt, pos),
        device_id_type=MESH,
    )

    @pl.when(sec == last)
    def _():
        normed = normalize(ybuf[...].astype(F32)).astype(BF16)
        predicted = jnp.dot(normed, read_buf[...], preferred_element_type=F32)
        upd[...] = (
            coef_ref[0, plan] * state_ref[0].astype(F32)
            + coef_ref[1, plan] * predicted
            + coef_ref[2, plan] * noise_ref[0].astype(F32)
        ).astype(BF16)
        upd_copy.start()

    state_copy.wait_recv()

    @pl.when(sec == 0)
    def _():
        member = ens_ref[pl.ds(slots_ref[last], 1), :]
        h_ref[0] = (
            jnp.dot(s_ref[0], lift_buf[...], preferred_element_type=F32) + member
        ).astype(BF16)

    @pl.when(sec != 0)
    def _():
        for piece in range(2):
            y_copy(piece).wait_recv()

    @pl.when(sec != last)
    def _():
        for piece in range(2):
            y_copy(piece).wait_send()

    state_copy.wait_send()

    @pl.when(at_hub)
    def _():
        for piece in range(2):
            for part in range(2):
                for index in range(peers):
                    o_copy(piece, index, part).wait_send()

    @pl.when(jnp.logical_not(at_hub))
    def _():
        for piece in range(2):
            x_copy(slot, piece).wait_send()


def place(h_in, s_in, h_out, s_out, sem):
    copies = [
        pltpu.make_async_copy(h_in, h_out, sem.at[0]),
        pltpu.make_async_copy(s_in, s_out, sem.at[1]),
    ]
    for copy in copies:
        copy.start()
    for copy in copies:
        copy.wait()


def body(
    n, sections,
    carried_activations,
    corrupted_field,
    gaussian_perturbation,
    timeline_entry_number,
    ensemble_slots,
    attention_entry_matrices,
    attention_exit_matrix,
    adaptive_norm_terms,
    score_multiplier,
    lifting_matrix,
    readout_matrix,
    ensemble_vectors,
    denoiser_coefficients,
):
    _, local, model = carried_activations.shape
    channels = corrupted_field.shape[2]
    width = attention_exit_matrix.shape[1]
    heads = score_multiplier.shape[1]
    half = local // 2
    pairs = heads // 2
    lanes = 2 * (width // heads)
    chunks = 3
    terms = adaptive_norm_terms.reshape(-1, 1, model)
    smem = pl.BlockSpec(memory_space=pltpu.SMEM)
    vmem = pl.BlockSpec(memory_space=pltpu.VMEM)
    hbm = pl.BlockSpec(memory_space=pl.ANY)
    def dma(*shape):
        return pltpu.SemaphoreType.DMA(shape)

    staged = [
        pltpu.VMEM(carried_activations.shape, BF16),
        pltpu.VMEM(corrupted_field.shape, BF16),
        pltpu.VMEM(gaussian_perturbation.shape, BF16),
        pltpu.VMEM(terms.shape, F32),
        pltpu.VMEM(ensemble_vectors.shape, F32),
    ]
    if n == 4 and sections % 2 == 0 and heads % 4 == 0 and local % 32 == 0:
        scalars = hbm
        run = functools.partial(hub_kernel, n, sections, heads)
        scratch = [
            pltpu.VMEM((model, 3 * width), BF16),
            pltpu.VMEM((width, model), BF16),
            pltpu.VMEM(lifting_matrix.shape, BF16),
            pltpu.VMEM(readout_matrix.shape, BF16),
            pltpu.VMEM((2, n - 1, half, model), BF16),
            pltpu.VMEM((local, model), BF16),
            pltpu.VMEM((n * local, width), BF16),
            pltpu.VMEM((pairs, n * local, 2 * lanes), BF16),
            pltpu.VMEM((n * local, width), BF16),
            pltpu.VMEM((2, n - 1, half, width), BF16),
            pltpu.VMEM((local, width), BF16),
            pltpu.VMEM((local, model), BF16),
            pltpu.VMEM((local, channels), BF16),
            *staged,
            pltpu.SMEM(timeline_entry_number.shape, jnp.int32),
            pltpu.SMEM(ensemble_slots.shape, jnp.int32),
            pltpu.SMEM(score_multiplier.shape, F32),
            pltpu.SMEM(denoiser_coefficients.shape[::-1], F32),
            dma(13), dma(2), dma(2, n - 1), dma(2, n - 1, 2), dma(2, 2), dma(2), dma(2),
            pltpu.SemaphoreType.DMA,
            pltpu.SemaphoreType.DMA,
        ]
    else:
        scalars = smem
        run = functools.partial(line_kernel, n, sections, heads, chunks)
        scratch = [
                pltpu.VMEM((3, model, width), BF16),
                pltpu.VMEM((width, model), BF16),
                pltpu.VMEM(lifting_matrix.shape, BF16),
                pltpu.VMEM(readout_matrix.shape, BF16),
                pltpu.VMEM((n, half, model), BF16),
                pltpu.VMEM((2, n, half, 2 * width), BF16),
                pltpu.VMEM((2, pairs, 2 * local, lanes), BF16),
                pltpu.VMEM((2, pairs, 2 * local, lanes), F32),
                pltpu.VMEM((2, pairs, 2 * local, 1), F32),
                pltpu.VMEM((2, pairs, 2 * local, 1), F32),
                pltpu.VMEM((local, width), BF16),
                pltpu.VMEM((chunks, local, model // chunks), BF16),
                pltpu.VMEM((local, channels), BF16),
                pltpu.VMEM((local, width), BF16),
                pltpu.VMEM((local, width), BF16),
                pltpu.VMEM((pairs, local, lanes), BF16),
                pltpu.VMEM((pairs, local, lanes), BF16),
                pltpu.VMEM(carried_activations.shape, BF16),
                pltpu.VMEM(corrupted_field.shape, BF16),
                pltpu.VMEM(gaussian_perturbation.shape, BF16),
                pltpu.VMEM(terms.shape, F32),
                pltpu.VMEM(ensemble_vectors.shape, F32),
                pltpu.SemaphoreType.DMA((11,)),
                pltpu.SemaphoreType.DMA((2, 2, n - 1)),
                pltpu.SemaphoreType.DMA((2, 2, n - 1)),
                pltpu.SemaphoreType.DMA((chunks,)),
                pltpu.SemaphoreType.DMA((chunks,)),
                pltpu.SemaphoreType.DMA,
                pltpu.SemaphoreType.DMA,
                pltpu.SemaphoreType.DMA,
                pltpu.SemaphoreType.DMA,
                pltpu.SemaphoreType.DMA((pairs,)),
                pltpu.SemaphoreType.DMA((pairs,)),
        ]
    stream, field = pl.pallas_call(
        run,
        out_shape=(
            pltpu.VMEM(carried_activations.shape, BF16),
            pltpu.VMEM(corrupted_field.shape, BF16),
        ),
        in_specs=[scalars] * 4 + [hbm] * 9,
        out_specs=(vmem, vmem),
        scratch_shapes=scratch,
        compiler_params=pltpu.CompilerParams(
            collective_id=0, has_side_effects=True, vmem_limit_bytes=60 * 1024 * 1024
        ),
        name="denoise_pass",
    )(
        timeline_entry_number,
        ensemble_slots,
        score_multiplier,
        denoiser_coefficients.T,
        carried_activations,
        corrupted_field,
        gaussian_perturbation,
        terms,
        ensemble_vectors,
        attention_entry_matrices,
        attention_exit_matrix,
        lifting_matrix,
        readout_matrix,
    )
    return pl.pallas_call(
        place,
        out_shape=(
            jax.ShapeDtypeStruct(stream.shape, BF16),
            jax.ShapeDtypeStruct(field.shape, BF16),
        ),
        in_specs=[vmem, vmem],
        out_specs=(hbm, hbm),
        scratch_shapes=[pltpu.SemaphoreType.DMA((2,))],
        name="place_results",
    )(
        pltpu.with_memory_space_constraint(stream, pltpu.VMEM),
        pltpu.with_memory_space_constraint(field, pltpu.VMEM),
    )


def solution(mesh):
    placed = (
        P("section", "tok", None),
        P("section", "tok", None),
        P(None, "tok", None),
        P(),
        P(),
        P("section", None, None),
        P("section", None, None),
        P("section", None, None, None),
        P("section", None),
        P(),
        P(),
        P(),
        P(),
    )
    return jax.shard_map(
        functools.partial(body, mesh.shape["tok"], mesh.shape["section"]),
        mesh=mesh,
        in_specs=placed,
        out_specs=(P("section", "tok", None), P("section", "tok", None)),
        check_vma=False,
    )
```
